512 devices in a mesh: section: 8 (over z_hi, core), ctx: 64 (over x, y, z_lo).
Axes of the slice: x: 4, y: 4, z: 16 (z_hi: 4, z_lo: 4; z = z_hi * 4 + z_lo), core: 2. Of those that a mesh axis runs over, the one named last changes fastest.
Arguments:
- down_queries: bfloat16 [8, 8192, 2304], P('section', 'ctx'), may hold values from -40 to 40
- down_keys: bfloat16 [8, 8192, 2304], P('section', 'ctx'), may hold values from -40 to 40
- down_values: bfloat16 [8, 8192, 2304], P('section', 'ctx'), may hold values from -6 to 6
- up_queries: bfloat16 [8, 8192, 2304], P('section', 'ctx'), may hold values from -40 to 40
- up_keys: bfloat16 [8, 8192, 2304], P('section', 'ctx'), may hold values from -40 to 40
- up_values: bfloat16 [8, 8192, 2304], P('section', 'ctx'), may hold values from -6 to 6
- key_blocks: int32 [64, 2], P('ctx'), may hold values from -1 to 47, as said below
Outputs:
- forward: bfloat16 [8, 8192, 2304], P('section', 'ctx')
- handed: bfloat16 [8, 8192, 2304], P('section', 'ctx')
The draws below stay inside these ranges and needn't reach their ends.
Inputs may be any that keep to these rules, and one draw needn't show every extreme that they name: `key_blocks`: slot k (counting from 1) of query block i holds i - k * 16 or -1, and -1 wherever i - k * 16 is negative.
All inputs are finite; a program needn't handle non-finite values.
Results may differ from the reference program's by a relative error of at most 0.0038.
Values may be sent and summed in bfloat16 or wider, within the bound.
A program may use at most 64 MiB of HBM per device.

```python
import math
import jax
import jax.numpy as jnp
from jax import lax

HEAD_DIM = 64
HEADS = 36
D = 2304
BLOCK = 128
NSTR = 2
TOKENS = 8192
NB = 64
STRIDE = 16
N_SECTION = 8


def draw_pair(key, salt):
    key = jax.random.fold_in(key, salt)
    subkeys = jax.random.split(key, 5)
    full_shape = (N_SECTION, TOKENS, D)
    query_scale = jnp.exp(jax.random.uniform(subkeys[3], (N_SECTION, TOKENS, 1), jnp.float32, 0.0, math.log(4.0)))
    key_scale = jnp.exp(jax.random.uniform(subkeys[4], (N_SECTION, TOKENS, 1), jnp.float32, 0.0, math.log(4.0)))
    query_rows = jax.random.normal(subkeys[0], full_shape, jnp.float32) * query_scale
    key_rows = jax.random.normal(subkeys[1], full_shape, jnp.float32) * key_scale
    return (jnp.clip(query_rows, -40.0, 40.0).astype(jnp.bfloat16), jnp.clip(key_rows, -40.0, 40.0).astype(jnp.bfloat16))


def draw_down_queries(key, part):
    return draw_pair(key, 11)[0]


def draw_down_keys(key, part):
    return draw_pair(key, 11)[1]


def draw_up_queries(key, part):
    return draw_pair(key, 23)[0]


def draw_up_keys(key, part):
    return draw_pair(key, 23)[1]


def draw_key_blocks(key, part):
    key = jax.random.fold_in(key, 41)
    block_ids = jnp.arange(NB, dtype=jnp.int32)[:, None]
    offset_steps = jnp.arange(1, NSTR + 1, dtype=jnp.int32)[None, :]
    target = block_ids - offset_steps * STRIDE
    keeping = jax.random.randint(key, (NB, NSTR), 0, 4) < 3
    keeping = keeping | (block_ids == NB - 1)
    return jnp.where((target >= 0) & keeping, target, -1).astype(jnp.int32)


def shard_levels(rng, shape, cuts, smallest, top_value):
    factor_of = 1.0
    for dim, parts in cuts:
        heights = jax.random.uniform(jax.random.fold_in(jax.random.fold_in(rng, 6), dim), (parts,), jnp.float32, smallest / len(cuts), top_value / len(cuts))
        factor_of = factor_of * jnp.repeat(jnp.exp(heights), shape[dim] // parts).reshape((-1,) + (1,) * (len(shape) - 1 - dim))
    return factor_of


def bell_draw(key, shape, spread, most, cuts=(), kind=jnp.bfloat16):
    result = jax.random.normal(key, shape, jnp.float32) * spread
    if len(cuts) > 0:
        result = shard_levels(key, shape, cuts, -0.22, 0.18) * result
    return jnp.clip(result, min=-most, max=most).astype(kind)


def setup_inputs(seed: int = 0) -> dict:
    seeds = jax.random.split(jax.random.key(seed), 8)
    return {
        "down_queries": draw_down_queries(jax.random.fold_in(seeds[7], 71), 0),
        "down_keys": draw_down_keys(jax.random.fold_in(seeds[7], 71), 0),
        "down_values": bell_draw(seeds[2], (N_SECTION, TOKENS, D), 1.0, 6.0, ((0, 8), (1, 64))),
        "up_queries": draw_up_queries(jax.random.fold_in(seeds[7], 71), 0),
        "up_keys": draw_up_keys(jax.random.fold_in(seeds[7], 71), 0),
        "up_values": bell_draw(seeds[5], (N_SECTION, TOKENS, D), 1.0, 6.0, ((0, 8), (1, 64))),
        "key_blocks": draw_key_blocks(jax.random.fold_in(seeds[7], 71), 0),
    }


def attention(query_in, key_in, value_in, key_blocks):
    queries = query_in.reshape(NB, BLOCK, HEADS, HEAD_DIM)
    key_rows = key_in.reshape(NB, BLOCK, HEADS, HEAD_DIM)
    value_rows = value_in.reshape(NB, BLOCK, HEADS, HEAD_DIM)
    causal = jnp.arange(BLOCK)[:, None] >= jnp.arange(BLOCK)[None, :]
    scale = 1.0 / math.sqrt(HEAD_DIM)

    def attend(block_index):
        listed = key_blocks[block_index]
        key_parts = [key_rows[block_index]]
        value_parts = [value_rows[block_index]]
        allowed = [causal]
        for offset_step in range(NSTR):
            source_block = jnp.maximum(listed[offset_step], 0).astype(jnp.int32)
            key_parts.append(key_rows[source_block])
            value_parts.append(value_rows[source_block])
            allowed.append(jnp.broadcast_to(listed[offset_step] >= 0, (BLOCK, BLOCK)))
        key_all = jnp.concatenate(key_parts, 0).astype(jnp.float32)
        value_all = jnp.concatenate(value_parts, 0).astype(jnp.float32)
        allowed_all = jnp.concatenate(allowed, 1)
        scores = jnp.einsum('qhd,khd->hqk', queries[block_index].astype(jnp.float32), key_all) * scale
        scores = jnp.where(allowed_all[None], scores, -1e+30)
        highest = lax.optimization_barrier(jnp.max(scores, -1, keepdims=True))
        expo = jnp.exp(scores - highest)
        weights = (expo / lax.optimization_barrier(jnp.sum(expo, -1, keepdims=True))).astype(jnp.bfloat16)
        return jnp.einsum('hqk,khd->qhd', weights.astype(jnp.float32), value_all)
    mixture = lax.map(attend, jnp.arange(NB, dtype=jnp.int32)).reshape(TOKENS, D)
    return mixture.astype(jnp.bfloat16)

def reference(down_queries, down_keys, down_values, up_queries, up_keys, up_values, key_blocks):
    lowered = [attention(down_queries[number], down_keys[number], down_values[number], key_blocks) for number in range(N_SECTION)]
    raised = [attention(up_queries[number], up_keys[number], up_values[number], key_blocks) for number in range(N_SECTION)]
    forward = jnp.stack([raised[0]] + lowered[:-1])
    handed = jnp.stack(raised[1:] + [lowered[-1]])
    return (forward, handed)
```

```python
import math

import jax
import jax.numpy as jnp
from jax import lax
from jax.experimental import pallas as pl
from jax.experimental.pallas import tpu as pltpu
from jax.sharding import PartitionSpec as P

HEAD_DIM = 64
PAIR = 2 * HEAD_DIM
PAIRS = 1
AHEAD = 4
RELAY = 2
LAG = 2
NEG = -1e30
FLOOR = -5e29
RATE = math.log2(math.e) / math.sqrt(HEAD_DIM)
MESH = pl.DeviceIdType.MESH


def kernel(sections, spacing, kb, dq, dk, dv, uq, uk, uv, fwd, hand, own, got, part_in, stat_in,
           part_out, stat_out, final, flag, flag_in, load_sem, data_send, data_recv, part_send,
           part_recv, stat_send, stat_recv, out_send, out_recv, flag_send, flag_recv):
    s = lax.axis_index("section")
    i = lax.axis_index("ctx")
    x = i // spacing
    rest = i - x * spacing
    right = (s, lax.rem(x + 1, 4) * spacing + rest)
    left = (s, lax.rem(x + 3, 4) * spacing + rest)
    below = (lax.max(s - 1, 0), i)
    above = (lax.min(s + 1, sections - 1), i)
    rows = own.shape[1]
    wide = PAIRS * PAIR
    steps = own.shape[2] // wide
    ins = (dq, dk, dv, uq, uk, uv)
    QD, KD, VD, QU, KU, VU = range(6)

    def lanes(c):
        return pl.ds(pl.multiple_of(c * wide, wide), wide)

    def remote(src, dst, send, recv, where):
        return pltpu.make_async_remote_copy(
            src_ref=src, dst_ref=dst, send_sem=send, recv_sem=recv, device_id=where,
            device_id_type=MESH)

    def data(k, c, src, r, where):
        return remote(src.at[:, lanes(c)], got.at[r, :, lanes(c)], data_send.at[k, c],
                      data_recv.at[r, c], where)

    def send_in(k, c, a, r, where):
        data(k, c, ins[a].at[0], r, where).start()

    def send_on(k, c, r0, r, where):
        data(k, c, got.at[r0], r, where).start()

    def wait_data(c, *slots):
        for r in slots:
            data(0, c, got.at[r], r, right).wait_recv()

    def parts(k, c, src, stat, r, where):
        return (remote(src.at[c], part_in.at[r, c], part_send.at[k, c], part_recv.at[r, c], where),
                remote(stat.at[c], stat_in.at[r, c], stat_send.at[k, c], stat_recv.at[r, c], where))

    def send_part(k, c, r, where):
        for copy in parts(k, c, part_out.at[k], stat_out.at[k], r, where):
            copy.start()

    def relay_part(k, c, r0, r, where):
        for copy in parts(k, c, part_in.at[r0], stat_in.at[r0], r, where):
            copy.start()

    def wait_part(c, *slots):
        for r in slots:
            for copy in parts(0, c, part_in.at[r], stat_in.at[r], r, right):
                copy.wait_recv()

    def out_remote(g, c):
        src = final.at[g, :, lanes(c)]
        dst = (fwd, hand)[g].at[0, :, lanes(c)]
        return remote(src, dst, out_send.at[g, c], out_recv.at[g, c], (above, below)[g])

    def out_local(g, c):
        dst = (hand, fwd)[g].at[0, :, lanes(c)]
        return pltpu.make_async_copy(final.at[g, :, lanes(c)], dst, out_send.at[g, c])

    def ends(g):
        return s == (sections - 1, 0)[g]

    def send_out(g, c):
        @pl.when(ends(g))
        def _():
            out_local(g, c).start()

        @pl.when(jnp.logical_not(ends(g)))
        def _():
            out_remote(g, c).start()

    lane = lax.broadcasted_iota(jnp.int32, (rows, PAIR), 1)
    row = lax.broadcasted_iota(jnp.int32, (PAIR, rows), 0)
    first = row < HEAD_DIM
    key = lax.broadcasted_iota(jnp.int32, (rows, 2 * rows), 0)
    query = lax.broadcasted_iota(jnp.int32, (rows, 2 * rows), 1)
    causal = key <= lax.rem(query, rows)

    def piece(ref, c, p):
        return ref[:, pl.ds(pl.multiple_of(c * wide + p * PAIR, PAIR), PAIR)]

    def spread(v):
        return jnp.where(first, v[:, :rows], v[:, rows:])

    def attend(q, sources):
        zero = jnp.zeros_like(q)
        both = jnp.concatenate([jnp.where(lane < HEAD_DIM, q, zero), jnp.where(lane < HEAD_DIM, zero, q)], 0)
        tops, scores, floored = [], [], True
        for k, v, bias, masked in sources:
            sc = lax.dot_general(k, both, (((1,), (1,)), ((), ())), preferred_element_type=jnp.float32)
            if masked:
                sc = jnp.where(causal, sc, NEG)
            top = jnp.max(sc, 0, keepdims=True)
            if bias is None:
                floored = False
            else:
                top = top + bias
            tops.append(top)
            scores.append(sc)
        high = tops[0]
        for top in tops[1:]:
            high = jnp.maximum(high, top)
        if floored:
            high = jnp.maximum(high, FLOOR)
        total, mixed = None, None
        for (k, v, bias, masked), sc in zip(sources, scores):
            base = high if bias is None else high - bias
            e = jnp.exp2((sc - base) * RATE)
            t = jnp.sum(e, 0, keepdims=True)
            o = lax.dot_general(v, e.astype(jnp.bfloat16), (((0,), (0,)), ((), ())),
                                preferred_element_type=jnp.float32)
            total = t if total is None else total + t
            mixed = o if mixed is None else mixed + o
        return jnp.where(first, mixed[:, :rows], mixed[:, rows:]), high, total

    def merge(items, floored=False):
        high = items[0][1]
        for item in items[1:]:
            high = jnp.maximum(high, item[1])
        if floored:
            high = jnp.maximum(high, FLOOR)
        mixed, total = None, None
        for o, top, t in items:
            w = jnp.exp2((top - high) * RATE)
            mixed = o * spread(w) if mixed is None else mixed + o * spread(w)
            total = t * w if total is None else total + t * w
        return mixed, high, total

    def keep(k, c, p, item):
        o, top, t = item
        part_out[k, c, pl.ds(p * PAIR, PAIR), :] = o.astype(jnp.bfloat16)
        at = 4 * p
        stat_out[k, c, pl.ds(at, 1), :] = top[:, :rows]
        stat_out[k, c, pl.ds(at + 1, 1), :] = top[:, rows:]
        stat_out[k, c, pl.ds(at + 2, 1), :] = t[:, :rows]
        stat_out[k, c, pl.ds(at + 3, 1), :] = t[:, rows:]

    def arrived(r, c, p, bias=None):
        o = part_in[r, c, pl.ds(p * PAIR, PAIR), :].astype(jnp.float32)
        at = 4 * p
        lines = [stat_in[r, c, pl.ds(at + n, 1), :] for n in range(4)]
        top = jnp.concatenate(lines[:2], 1)
        if bias is not None:
            top = top + bias
        return o, top, jnp.concatenate(lines[2:], 1)

    def finish(g, c, p, item):
        o, top, t = item
        o = o * spread(1.0 / t)
        final[g, :, pl.ds(pl.multiple_of(c * wide + p * PAIR, PAIR), PAIR)] = o.T.astype(jnp.bfloat16)

    def mine(a, c, p):
        return piece(own.at[a], c, p)

    def sent(r, c, p):
        return piece(got.at[r], c, p)

    def self_part(g, c, p):
        q, k, v = (mine(3 * g + n, c, p) for n in range(3))
        return attend(q, [(k, v, None, True)])

    def own_bias(slot):
        return flag[pl.ds(slot, 1), :]

    def far_bias(slot):
        return flag_in[pl.ds(slot, 1), :]

    loads = [pltpu.make_async_copy(ins[a].at[0], own.at[a], load_sem.at[a]) for a in range(6)]
    for copy in loads:
        copy.start()
    bias = [jnp.where(kb[0, n] >= 0, 0.0, NEG) for n in range(2)]
    flag_row = lax.broadcasted_iota(jnp.int32, flag.shape, 0)
    flag[...] = jnp.where(flag_row == 0, bias[0], bias[1])

    barrier = pltpu.get_barrier_semaphore()
    for where in (left, right):
        pl.semaphore_signal(barrier, inc=1, device_id=where, device_id_type=MESH)

    @pl.when(s > 0)
    def _():
        pl.semaphore_signal(barrier, inc=1, device_id=below, device_id_type=MESH)

    @pl.when(s < sections - 1)
    def _():
        pl.semaphore_signal(barrier, inc=1, device_id=above, device_id_type=MESH)

    edges = jnp.where(s > 0, 1, 0) + jnp.where(s < sections - 1, 1, 0)
    pl.semaphore_wait(barrier, 2 + edges)

    def flags(k, src, where):
        return remote(src, flag_in, flag_send.at[k], flag_recv.at[0], where)

    def wait_loads():
        for copy in loads:
            copy.wait()

    def ahead(send):
        def go(c, carry):
            send(c)
            return carry

        lax.fori_loop(0, min(AHEAD, steps), go, 0)

    def run(extra, body):
        def go(t, carry):
            body(t)
            return carry

        lax.fori_loop(0, steps + extra, go, 0)

    def when_chunk(c, act):
        @pl.when(jnp.logical_and(c >= 0, c < steps))
        def _():
            act(c)

    def settle(n_data, n_part):
        def go(c, carry):
            for k in range(n_data):
                data(k, c, got.at[0], 0, right).wait_send()
            for k in range(n_part):
                for copy in parts(k, c, part_out.at[k], stat_out.at[k], 0, right):
                    copy.wait_send()
            return carry

        lax.fori_loop(0, steps, go, 0)

    @pl.when(x == 0)
    def _():
        def send(c):
            send_in(0, c, KD, 0, right)
            send_in(1, c, VD, 1, right)

        ahead(send)
        wait_loads()
        flags(0, flag, right).wait_recv()

        def hub(c):
            for p in range(PAIRS):
                finish(0, c, p, self_part(0, c, p))
                finish(1, c, p, self_part(1, c, p))
            wait_data(c, 0, 1, 2, 3, 4)
            for p in range(PAIRS):
                k0, v0 = mine(KU, c, p), mine(VU, c, p)
                k1, v1 = sent(0, c, p), sent(1, c, p)
                keep(1, c, p, attend(sent(3, c, p), [(k1, v1, far_bias(0), False), (k0, v0, far_bias(1), False)]))
                keep(2, c, p, attend(sent(4, c, p), [(k1, v1, None, False)]))
                keep(0, c, p, attend(sent(2, c, p), [(k0, v0, None, False)]))
            send_out(0, c)
            send_out(1, c)
            send_part(1, c, 3, left)
            send_part(2, c, 2, left)
            send_part(0, c, 0, right)

        def body(t):
            when_chunk(t + AHEAD, send)
            hub(t)

        run(0, body)
        settle(2, 3)

    @pl.when(x == 1)
    def _():
        def send(c):
            send_in(0, c, KU, 0, left)
            send_in(1, c, VU, 1, left)
            send_in(2, c, QU, 2, left)

        ahead(send)
        wait_loads()
        flags(0, flag, right).wait_recv()

        def hub(c):
            wait_data(c, 0, 1, 2, 3)
            for p in range(PAIRS):
                k1, v1 = mine(KD, c, p), mine(VD, c, p)
                k0, v0 = sent(0, c, p), sent(1, c, p)
                keep(1, c, p, attend(sent(3, c, p), [(k1, v1, None, False)]))
                keep(0, c, p, attend(sent(2, c, p), [(k1, v1, far_bias(0), False), (k0, v0, far_bias(1), False)]))
                finish(0, c, p, attend(mine(QD, c, p), [(k1, v1, None, True), (k0, v0, own_bias(0), False)]))
            send_part(1, c, 1, right)
            send_part(0, c, 0, right)
            send_out(0, c)

        def close(c):
            wait_part(c, 0)
            for p in range(PAIRS):
                finish(1, c, p, merge([self_part(1, c, p), arrived(0, c, p, own_bias(0))]))
            send_out(1, c)

        def body(t):
            when_chunk(t + AHEAD, send)
            when_chunk(t, hub)
            when_chunk(t - LAG, close)

        run(LAG, body)
        settle(3, 2)

    @pl.when(x == 2)
    def _():
        flags(0, flag, left).start()
        flags(1, flag, right).start()

        def send(c):
            send_in(0, c, QD, 2, left)
            send_in(1, c, QU, 0, right)

        ahead(send)

        def relay(c):
            wait_data(c, 0)
            send_on(2, c, 0, 3, left)

        for c in range(min(RELAY, steps)):
            relay(c)
        wait_loads()
        flags(0, flag, right).wait_recv()

        def side(c):
            wait_data(c, 1)
            for p in range(PAIRS):
                keep(1, c, p, attend(sent(1, c, p), [(mine(KU, c, p), mine(VU, c, p), None, False)]))
            send_part(1, c, 1, right)

        def middle(c):
            wait_part(c, 0, 1)
            for p in range(PAIRS):
                near = attend(sent(0, c, p), [(mine(KD, c, p), mine(VD, c, p), far_bias(0), False)])
                keep(0, c, p, merge([near, arrived(1, c, p, far_bias(1))], True))
                finish(0, c, p, merge([self_part(0, c, p), arrived(0, c, p)]))
            send_part(0, c, 0, right)
            send_out(0, c)

        def close(c):
            wait_part(c, 2)
            for p in range(PAIRS):
                finish(1, c, p, merge([self_part(1, c, p), arrived(2, c, p)]))
            send_out(1, c)

        def body(t):
            when_chunk(t + AHEAD, send)
            when_chunk(t + RELAY, relay)
            when_chunk(t, side)
            when_chunk(t - LAG, middle)
            when_chunk(t - 2 * LAG, close)

        run(2 * LAG, body)
        settle(3, 2)
        for k in range(2):
            flags(k, flag, right).wait_send()

    @pl.when(x == 3)
    def _():
        flags(0, flag, left).start()

        def send(c):
            send_in(0, c, QD, 0, left)
            send_in(1, c, QU, 1, left)
            send_in(2, c, QU, 4, right)

        ahead(send)
        flags(0, flag, right).wait_recv()
        flags(1, flag_in, right).start()

        def relay(c):
            wait_data(c, 0)
            send_on(3, c, 0, 3, right)

        for c in range(min(RELAY, steps)):
            relay(c)
        wait_loads()

        def middle(c):
            wait_part(c, 3)
            relay_part(0, c, 3, 2, left)
            wait_part(c, 1, 2)
            for p in range(PAIRS):
                items = [self_part(1, c, p), arrived(1, c, p, own_bias(0)), arrived(2, c, p, own_bias(1))]
                finish(1, c, p, merge(items))
            send_out(1, c)

        def close(c):
            wait_part(c, 0)
            for p in range(PAIRS):
                finish(0, c, p, merge([self_part(0, c, p), arrived(0, c, p)]))
            send_out(0, c)

        def body(t):
            when_chunk(t + AHEAD, send)
            when_chunk(t + RELAY, relay)
            when_chunk(t - LAG, middle)
            when_chunk(t - 2 * LAG, close)

        run(2 * LAG, body)
        settle(4, 1)
        for k in range(2):
            flags(k, flag, right).wait_send()

    for g in range(2):
        def done(c, carry, g=g):
            @pl.when(ends(g))
            def _():
                out_local(g, c).wait()

            @pl.when(jnp.logical_not(ends(g)))
            def _():
                out_remote(g, c).wait_send()

            @pl.when(jnp.logical_not(ends(1 - g)))
            def _():
                out_remote(g, c).wait_recv()

            return carry

        lax.fori_loop(0, steps, done, 0)


def solution(mesh):
    sections, spacing = mesh.shape["section"], mesh.shape["ctx"] // 4

    def on_device(dq, dk, dv, uq, uk, uv, key_blocks):
        _, rows, width = dq.shape
        wide = PAIRS * PAIR
        steps = width // wide
        half, full = jnp.bfloat16, jnp.float32
        dma = pltpu.SemaphoreType.DMA
        whole = pl.BlockSpec(memory_space=pl.ANY)
        out = jax.ShapeDtypeStruct(dq.shape, half)

        def body(*refs):
            kernel(sections, spacing, *refs)

        return pl.pallas_call(
            body,
            out_shape=(out, out),
            in_specs=[pl.BlockSpec(memory_space=pltpu.SMEM)] + [whole] * 6,
            out_specs=(whole, whole),
            scratch_shapes=[
                pltpu.VMEM((6, rows, width), half),
                pltpu.VMEM((5, rows, width), half),
                pltpu.VMEM((4, steps, wide, rows), half),
                pltpu.VMEM((4, steps, 8, rows), full),
                pltpu.VMEM((3, steps, wide, rows), half),
                pltpu.VMEM((3, steps, 8, rows), full),
                pltpu.VMEM((2, rows, width), half),
                pltpu.VMEM((8, 2 * rows), full),
                pltpu.VMEM((8, 2 * rows), full),
                dma((6,)),
                dma((4, steps)),
                dma((5, steps)),
                dma((3, steps)),
                dma((4, steps)),
                dma((3, steps)),
                dma((4, steps)),
                dma((2, steps)),
                dma((2, steps)),
                dma((2,)),
                dma((1,)),
            ],
            compiler_params=pltpu.CompilerParams(
                collective_id=0, has_side_effects=True, vmem_limit_bytes=40 * 1024 * 1024),
        )(key_blocks, dq, dk, dv, uq, uk, uv)

    placed = (P("section", "ctx", None),) * 6 + (P("ctx", None),)
    return jax.shard_map(
        on_device,
        mesh=mesh,
        in_specs=placed,
        out_specs=(P("section", "ctx", None), P("section", "ctx", None)),
        check_vma=False,
    )
```

```python
import math

import jax
import jax.numpy as jnp
from jax import lax
from jax.experimental import pallas as pl
from jax.experimental.pallas import tpu as pltpu
from jax.sharding import PartitionSpec as P

HEAD_DIM = 64
PAIR = 2 * HEAD_DIM
PAIRS = 1
AHEAD = 6
RELAY = 3
LAG = 2
NEG = -1e30
FLOOR = -5e29
RATE = math.log2(math.e) / math.sqrt(HEAD_DIM)
MESH = pl.DeviceIdType.MESH


def kernel(sections, spacing, kb, dq, dk, dv, uq, uk, uv, fwd, hand, own, got, part_in, stat_in,
           part_out, stat_out, final, flag, flag_in, load_sem, data_send, data_recv, part_send,
           part_recv, stat_send, stat_recv, out_send, out_recv, flag_send, flag_recv):
    s = lax.axis_index("section")
    i = lax.axis_index("ctx")
    x = i // spacing
    rest = i - x * spacing
    right = (s, lax.rem(x + 1, 4) * spacing + rest)
    left = (s, lax.rem(x + 3, 4) * spacing + rest)
    below = (lax.max(s - 1, 0), i)
    above = (lax.min(s + 1, sections - 1), i)
    rows = own.shape[1]
    wide = PAIRS * PAIR
    steps = own.shape[2] // wide
    ins = (dq, dk, dv, uq, uk, uv)
    QD, KD, VD, QU, KU, VU = range(6)

    def lanes(c):
        return pl.ds(pl.multiple_of(c * wide, wide), wide)

    def remote(src, dst, send, recv, where):
        return pltpu.make_async_remote_copy(
            src_ref=src, dst_ref=dst, send_sem=send, recv_sem=recv, device_id=where,
            device_id_type=MESH)

    def data(k, c, src, r, where):
        return remote(src.at[:, lanes(c)], got.at[r, :, lanes(c)], data_send.at[k, c],
                      data_recv.at[r, c], where)

    def send_in(k, c, a, r, where):
        data(k, c, ins[a].at[0], r, where).start()

    def send_on(k, c, r0, r, where):
        data(k, c, got.at[r0], r, where).start()

    def wait_data(c, *slots):
        for r in slots:
            data(0, c, got.at[r], r, right).wait_recv()

    def parts(k, c, src, stat, r, where):
        return (remote(src.at[c], part_in.at[r, c], part_send.at[k, c], part_recv.at[r, c], where),
                remote(stat.at[c], stat_in.at[r, c], stat_send.at[k, c], stat_recv.at[r, c], where))

    def send_part(k, c, r, where):
        for copy in parts(k, c, part_out.at[k], stat_out.at[k], r, where):
            copy.start()

    def relay_part(k, c, r0, r, where):
        for copy in parts(k, c, part_in.at[r0], stat_in.at[r0], r, where):
            copy.start()

    def wait_part(c, *slots):
        for r in slots:
            for copy in parts(0, c, part_in.at[r], stat_in.at[r], r, right):
                copy.wait_recv()

    def out_remote(g, c):
        src = final.at[g, :, lanes(c)]
        dst = (fwd, hand)[g].at[0, :, lanes(c)]
        return remote(src, dst, out_send.at[g, c], out_recv.at[g, c], (above, below)[g])

    def out_local(g, c):
        dst = (hand, fwd)[g].at[0, :, lanes(c)]
        return pltpu.make_async_copy(final.at[g, :, lanes(c)], dst, out_send.at[g, c])

    def ends(g):
        return s == (sections - 1, 0)[g]

    def send_out(g, c):
        @pl.when(ends(g))
        def _():
            out_local(g, c).start()

        @pl.when(jnp.logical_not(ends(g)))
        def _():
            out_remote(g, c).start()

    lane = lax.broadcasted_iota(jnp.int32, (rows, PAIR), 1)
    row = lax.broadcasted_iota(jnp.int32, (PAIR, rows), 0)
    first = row < HEAD_DIM
    key = lax.broadcasted_iota(jnp.int32, (rows, 2 * rows), 0)
    query = lax.broadcasted_iota(jnp.int32, (rows, 2 * rows), 1)
    causal = key <= lax.rem(query, rows)

    def piece(ref, c, p):
        return ref[:, pl.ds(pl.multiple_of(c * wide + p * PAIR, PAIR), PAIR)]

    def spread(v):
        return jnp.where(first, v[:, :rows], v[:, rows:])

    def attend(q, sources):
        zero = jnp.zeros_like(q)
        both = jnp.concatenate([jnp.where(lane < HEAD_DIM, q, zero), jnp.where(lane < HEAD_DIM, zero, q)], 0)
        tops, scores, floored = [], [], True
        for k, v, bias, masked in sources:
            sc = lax.dot_general(k, both, (((1,), (1,)), ((), ())), preferred_element_type=jnp.float32)
            if masked:
                sc = jnp.where(causal, sc, NEG)
            top = jnp.max(sc, 0, keepdims=True)
            if bias is None:
                floored = False
            else:
                top = top + bias
            tops.append(top)
            scores.append(sc)
        high = tops[0]
        for top in tops[1:]:
            high = jnp.maximum(high, top)
        if floored:
            high = jnp.maximum(high, FLOOR)
        total, mixed = None, None
        for (k, v, bias, masked), sc in zip(sources, scores):
            base = high if bias is None else high - bias
            e = jnp.exp2((sc - base) * RATE)
            t = jnp.sum(e, 0, keepdims=True)
            o = lax.dot_general(v, e.astype(jnp.bfloat16), (((0,), (0,)), ((), ())),
                                preferred_element_type=jnp.float32)
            total = t if total is None else total + t
            mixed = o if mixed is None else mixed + o
        return jnp.where(first, mixed[:, :rows], mixed[:, rows:]), high, total

    def merge(items, floored=False):
        high = items[0][1]
        for item in items[1:]:
            high = jnp.maximum(high, item[1])
        if floored:
            high = jnp.maximum(high, FLOOR)
        mixed, total = None, None
        for o, top, t in items:
            w = jnp.exp2((top - high) * RATE)
            mixed = o * spread(w) if mixed is None else mixed + o * spread(w)
            total = t * w if total is None else total + t * w
        return mixed, high, total

    def keep(k, c, p, item):
        o, top, t = item
        part_out[k, c, pl.ds(p * PAIR, PAIR), :] = o.astype(jnp.bfloat16)
        at = 4 * p
        stat_out[k, c, pl.ds(at, 1), :] = top[:, :rows]
        stat_out[k, c, pl.ds(at + 1, 1), :] = top[:, rows:]
        stat_out[k, c, pl.ds(at + 2, 1), :] = t[:, :rows]
        stat_out[k, c, pl.ds(at + 3, 1), :] = t[:, rows:]

    def arrived(r, c, p, bias=None):
        o = part_in[r, c, pl.ds(p * PAIR, PAIR), :].astype(jnp.float32)
        at = 4 * p
        lines = [stat_in[r, c, pl.ds(at + n, 1), :] for n in range(4)]
        top = jnp.concatenate(lines[:2], 1)
        if bias is not None:
            top = top + bias
        return o, top, jnp.concatenate(lines[2:], 1)

    def finish(g, c, p, item):
        o, top, t = item
        o = o * spread(1.0 / t)
        final[g, :, pl.ds(pl.multiple_of(c * wide + p * PAIR, PAIR), PAIR)] = o.T.astype(jnp.bfloat16)

    def mine(a, c, p):
        return piece(own.at[a], c, p)

    def sent(r, c, p):
        return piece(got.at[r], c, p)

    def self_part(g, c, p):
        q, k, v = (mine(3 * g + n, c, p) for n in range(3))
        return attend(q, [(k, v, None, True)])

    def own_bias(slot):
        return flag[pl.ds(slot, 1), :]

    def far_bias(slot):
        return flag_in[pl.ds(slot, 1), :]

    loads = [pltpu.make_async_copy(ins[a].at[0], own.at[a], load_sem.at[a]) for a in range(6)]
    for copy in loads:
        copy.start()
    bias = [jnp.where(kb[0, n] >= 0, 0.0, NEG) for n in range(2)]
    flag_row = lax.broadcasted_iota(jnp.int32, flag.shape, 0)
    flag[...] = jnp.where(flag_row == 0, bias[0], bias[1])

    barrier = pltpu.get_barrier_semaphore()
    for where in (left, right):
        pl.semaphore_signal(barrier, inc=1, device_id=where, device_id_type=MESH)

    @pl.when(s > 0)
    def _():
        pl.semaphore_signal(barrier, inc=1, device_id=below, device_id_type=MESH)

    @pl.when(s < sections - 1)
    def _():
        pl.semaphore_signal(barrier, inc=1, device_id=above, device_id_type=MESH)

    edges = jnp.where(s > 0, 1, 0) + jnp.where(s < sections - 1, 1, 0)
    pl.semaphore_wait(barrier, 2 + edges)

    def flags(k, src, where):
        return remote(src, flag_in, flag_send.at[k], flag_recv.at[0], where)

    def wait_loads():
        for copy in loads:
            copy.wait()

    def ahead(send):
        def go(c, carry):
            send(c)
            return carry

        lax.fori_loop(0, min(AHEAD, steps), go, 0)

    def run(extra, body):
        def go(t, carry):
            body(t)
            return carry

        lax.fori_loop(0, steps + extra, go, 0)

    def when_chunk(c, act):
        @pl.when(jnp.logical_and(c >= 0, c < steps))
        def _():
            act(c)

    def settle(n_data, n_part):
        def go(c, carry):
            for k in range(n_data):
                data(k, c, got.at[0], 0, right).wait_send()
            for k in range(n_part):
                for copy in parts(k, c, part_out.at[k], stat_out.at[k], 0, right):
                    copy.wait_send()
            return carry

        lax.fori_loop(0, steps, go, 0)

    @pl.when(x == 0)
    def _():
        def send(c):
            send_in(0, c, KD, 0, right)
            send_in(1, c, VD, 1, right)

        ahead(send)
        wait_loads()
        flags(0, flag, right).wait_recv()

        def hub(c):
            wait_data(c, 0, 1, 2, 3, 4)
            for p in range(PAIRS):
                k0, v0 = mine(KU, c, p), mine(VU, c, p)
                k1, v1 = sent(0, c, p), sent(1, c, p)
                keep(1, c, p, attend(sent(3, c, p), [(k1, v1, far_bias(0), False), (k0, v0, far_bias(1), False)]))
            send_part(1, c, 3, left)
            for p in range(PAIRS):
                keep(2, c, p, attend(sent(4, c, p), [(sent(0, c, p), sent(1, c, p), None, False)]))
            send_part(2, c, 2, left)
            for p in range(PAIRS):
                keep(0, c, p, attend(sent(2, c, p), [(mine(KU, c, p), mine(VU, c, p), None, False)]))
            send_part(0, c, 0, right)
            for p in range(PAIRS):
                finish(1, c, p, self_part(1, c, p))
                finish(0, c, p, self_part(0, c, p))
            send_out(1, c)
            send_out(0, c)

        def body(t):
            when_chunk(t + AHEAD, send)
            hub(t)

        run(0, body)
        settle(2, 3)

    @pl.when(x == 1)
    def _():
        def send(c):
            send_in(0, c, KU, 0, left)
            send_in(1, c, VU, 1, left)
            send_in(2, c, QU, 2, left)

        ahead(send)
        wait_loads()
        flags(0, flag, right).wait_recv()

        def hub(c):
            wait_data(c, 0, 1, 2, 3)
            for p in range(PAIRS):
                keep(1, c, p, attend(sent(3, c, p), [(mine(KD, c, p), mine(VD, c, p), None, False)]))
            send_part(1, c, 1, right)
            for p in range(PAIRS):
                k1, v1 = mine(KD, c, p), mine(VD, c, p)
                k0, v0 = sent(0, c, p), sent(1, c, p)
                keep(0, c, p, attend(sent(2, c, p), [(k1, v1, far_bias(0), False), (k0, v0, far_bias(1), False)]))
            send_part(0, c, 0, right)
            for p in range(PAIRS):
                k1, v1 = mine(KD, c, p), mine(VD, c, p)
                k0, v0 = sent(0, c, p), sent(1, c, p)
                finish(0, c, p, attend(mine(QD, c, p), [(k1, v1, None, True), (k0, v0, own_bias(0), False)]))
            send_out(0, c)

        def close(c):
            own_part = [self_part(1, c, p) for p in range(PAIRS)]
            wait_part(c, 0)
            for p in range(PAIRS):
                finish(1, c, p, merge([own_part[p], arrived(0, c, p, own_bias(0))]))
            send_out(1, c)

        def body(t):
            when_chunk(t + AHEAD, send)
            when_chunk(t, hub)
            when_chunk(t - LAG, close)

        run(LAG, body)
        settle(3, 2)

    @pl.when(x == 2)
    def _():
        flags(0, flag, left).start()
        flags(1, flag, right).start()

        def send(c):
            send_in(0, c, QD, 2, left)
            send_in(1, c, QU, 0, right)

        ahead(send)

        def relay(c):
            wait_data(c, 0)
            send_on(2, c, 0, 3, left)

        for c in range(min(RELAY, steps)):
            relay(c)
        wait_loads()
        flags(0, flag, right).wait_recv()

        def side(c):
            wait_data(c, 1)
            for p in range(PAIRS):
                keep(1, c, p, attend(sent(1, c, p), [(mine(KU, c, p), mine(VU, c, p), None, False)]))
            send_part(1, c, 1, right)

        def middle(c):
            near = [attend(sent(0, c, p), [(mine(KD, c, p), mine(VD, c, p), far_bias(0), False)])
                    for p in range(PAIRS)]
            wait_part(c, 1)
            for p in range(PAIRS):
                keep(0, c, p, merge([near[p], arrived(1, c, p, far_bias(1))], True))
            send_part(0, c, 0, right)
            own_part = [self_part(0, c, p) for p in range(PAIRS)]
            wait_part(c, 0)
            for p in range(PAIRS):
                finish(0, c, p, merge([own_part[p], arrived(0, c, p)]))
            send_out(0, c)

        def close(c):
            own_part = [self_part(1, c, p) for p in range(PAIRS)]
            wait_part(c, 2)
            for p in range(PAIRS):
                finish(1, c, p, merge([own_part[p], arrived(2, c, p)]))
            send_out(1, c)

        def body(t):
            when_chunk(t + AHEAD, send)
            when_chunk(t + RELAY, relay)
            when_chunk(t, side)
            when_chunk(t - LAG, middle)
            when_chunk(t - 2 * LAG, close)

        run(2 * LAG, body)
        settle(3, 2)
        for k in range(2):
            flags(k, flag, right).wait_send()

    @pl.when(x == 3)
    def _():
        flags(0, flag, left).start()

        def send(c):
            send_in(0, c, QD, 0, left)
            send_in(1, c, QU, 1, left)
            send_in(2, c, QU, 4, right)

        ahead(send)
        flags(0, flag, right).wait_recv()
        flags(1, flag_in, right).start()

        def relay(c):
            wait_data(c, 0)
            send_on(3, c, 0, 3, right)

        for c in range(min(RELAY, steps)):
            relay(c)
        wait_loads()

        def middle(c):
            wait_part(c, 3)
            relay_part(0, c, 3, 2, left)
            own_part = [self_part(1, c, p) for p in range(PAIRS)]
            wait_part(c, 1, 2)
            for p in range(PAIRS):
                items = [own_part[p], arrived(1, c, p, own_bias(0)), arrived(2, c, p, own_bias(1))]
                finish(1, c, p, merge(items))
            send_out(1, c)

        def close(c):
            own_part = [self_part(0, c, p) for p in range(PAIRS)]
            wait_part(c, 0)
            for p in range(PAIRS):
                finish(0, c, p, merge([own_part[p], arrived(0, c, p)]))
            send_out(0, c)

        def body(t):
            when_chunk(t + AHEAD, send)
            when_chunk(t + RELAY, relay)
            when_chunk(t - LAG, middle)
            when_chunk(t - 2 * LAG, close)

        run(2 * LAG, body)
        settle(4, 1)
        for k in range(2):
            flags(k, flag, right).wait_send()

    for g in range(2):
        def done(c, carry, g=g):
            @pl.when(ends(g))
            def _():
                out_local(g, c).wait()

            @pl.when(jnp.logical_not(ends(g)))
            def _():
                out_remote(g, c).wait_send()

            @pl.when(jnp.logical_not(ends(1 - g)))
            def _():
                out_remote(g, c).wait_recv()

            return carry

        lax.fori_loop(0, steps, done, 0)


def solution(mesh):
    sections, spacing = mesh.shape["section"], mesh.shape["ctx"] // 4

    def on_device(dq, dk, dv, uq, uk, uv, key_blocks):
        _, rows, width = dq.shape
        wide = PAIRS * PAIR
        steps = width // wide
        half, full = jnp.bfloat16, jnp.float32
        dma = pltpu.SemaphoreType.DMA
        whole = pl.BlockSpec(memory_space=pl.ANY)
        out = jax.ShapeDtypeStruct(dq.shape, half)

        def body(*refs):
            kernel(sections, spacing, *refs)

        return pl.pallas_call(
            body,
            out_shape=(out, out),
            in_specs=[pl.BlockSpec(memory_space=pltpu.SMEM)] + [whole] * 6,
            out_specs=(whole, whole),
            scratch_shapes=[
                pltpu.VMEM((6, rows, width), half),
                pltpu.VMEM((5, rows, width), half),
                pltpu.VMEM((4, steps, wide, rows), half),
                pltpu.VMEM((4, steps, 4 * PAIRS, rows), full),
                pltpu.VMEM((3, steps, wide, rows), half),
                pltpu.VMEM((3, steps, 4 * PAIRS, rows), full),
                pltpu.VMEM((2, rows, width), half),
                pltpu.VMEM((8, 2 * rows), full),
                pltpu.VMEM((8, 2 * rows), full),
                dma((6,)),
                dma((4, steps)),
                dma((5, steps)),
                dma((3, steps)),
                dma((4, steps)),
                dma((3, steps)),
                dma((4, steps)),
                dma((2, steps)),
                dma((2, steps)),
                dma((2,)),
                dma((1,)),
            ],
            compiler_params=pltpu.CompilerParams(
                collective_id=0, has_side_effects=True, vmem_limit_bytes=67043328),
        )(key_blocks, dq, dk, dv, uq, uk, uv)

    placed = (P("section", "ctx", None),) * 6 + (P("ctx", None),)
    return jax.shard_map(
        on_device,
        mesh=mesh,
        in_specs=placed,
        out_specs=(P("section", "ctx", None), P("section", "ctx", None)),
        check_vma=False,
    )
```

```python
import math

import jax
import jax.numpy as jnp
from jax import lax
from jax.experimental import pallas as pl
from jax.experimental.pallas import tpu as pltpu
from jax.sharding import PartitionSpec as P

HEAD_DIM = 64
PAIR = 2 * HEAD_DIM
PAIRS = 1
AHEAD = 8
NEAR = 4
RELAY = 4
LAG = 3
SKEW = 6
NEG = -1e30
FLOOR = -5e29
RATE = math.log2(math.e) / math.sqrt(HEAD_DIM)
MESH = pl.DeviceIdType.MESH


def kernel(sections, spacing, kb, dq, dk, dv, uq, uk, uv, fwd, hand, own, got, part_in, stat_in,
           part_out, stat_out, final, flag, flag_in, load_sem, data_send, data_recv, part_send,
           part_recv, stat_send, stat_recv, out_send, out_recv, flag_send, flag_recv):
    s = lax.axis_index("section")
    i = lax.axis_index("ctx")
    x = i // spacing
    rest = i - x * spacing
    right = (s, lax.rem(x + 1, 4) * spacing + rest)
    left = (s, lax.rem(x + 3, 4) * spacing + rest)
    below = (lax.max(s - 1, 0), i)
    above = (lax.min(s + 1, sections - 1), i)
    rows = own.shape[1]
    wide = PAIRS * PAIR
    steps = own.shape[2] // wide
    ins = (dq, dk, dv, uq, uk, uv)
    QD, KD, VD, QU, KU, VU = range(6)

    def lanes(c):
        return pl.ds(pl.multiple_of(c * wide, wide), wide)

    def remote(src, dst, send, recv, where):
        return pltpu.make_async_remote_copy(
            src_ref=src, dst_ref=dst, send_sem=send, recv_sem=recv, device_id=where,
            device_id_type=MESH)

    def data(k, c, src, r, where):
        return remote(src.at[:, lanes(c)], got.at[r, :, lanes(c)], data_send.at[k, c],
                      data_recv.at[r, c], where)

    def send_in(k, c, a, r, where):
        data(k, c, ins[a].at[0], r, where).start()

    def send_on(k, c, r0, r, where):
        data(k, c, got.at[r0], r, where).start()

    def wait_data(c, *slots):
        for r in slots:
            data(0, c, got.at[r], r, right).wait_recv()

    def parts(k, c, src, stat, r, where):
        return (remote(src.at[c], part_in.at[r, c], part_send.at[k, c], part_recv.at[r, c], where),
                remote(stat.at[c], stat_in.at[r, c], stat_send.at[k, c], stat_recv.at[r, c], where))

    def send_part(k, c, r, where):
        for copy in parts(k, c, part_out.at[k], stat_out.at[k], r, where):
            copy.start()

    def relay_part(k, c, r0, r, where):
        for copy in parts(k, c, part_in.at[r0], stat_in.at[r0], r, where):
            copy.start()

    def wait_part(c, *slots):
        for r in slots:
            for copy in parts(0, c, part_in.at[r], stat_in.at[r], r, right):
                copy.wait_recv()

    def out_remote(g, c):
        src = final.at[g, :, lanes(c)]
        dst = (fwd, hand)[g].at[0, :, lanes(c)]
        return remote(src, dst, out_send.at[g, c], out_recv.at[g, c], (above, below)[g])

    def out_local(g, c):
        dst = (hand, fwd)[g].at[0, :, lanes(c)]
        return pltpu.make_async_copy(final.at[g, :, lanes(c)], dst, out_send.at[g, c])

    def ends(g):
        return s == (sections - 1, 0)[g]

    def send_out(g, c):
        @pl.when(ends(g))
        def _():
            out_local(g, c).start()

        @pl.when(jnp.logical_not(ends(g)))
        def _():
            out_remote(g, c).start()

    lane = lax.broadcasted_iota(jnp.int32, (rows, PAIR), 1)
    row = lax.broadcasted_iota(jnp.int32, (PAIR, rows), 0)
    first = row < HEAD_DIM
    key = lax.broadcasted_iota(jnp.int32, (rows, 2 * rows), 0)
    query = lax.broadcasted_iota(jnp.int32, (rows, 2 * rows), 1)
    causal = key <= lax.rem(query, rows)

    def piece(ref, c, p):
        return ref[:, pl.ds(pl.multiple_of(c * wide + p * PAIR, PAIR), PAIR)]

    def spread(v):
        return jnp.where(first, v[:, :rows], v[:, rows:])

    def attend(q, sources):
        zero = jnp.zeros_like(q)
        both = jnp.concatenate([jnp.where(lane < HEAD_DIM, q, zero), jnp.where(lane < HEAD_DIM, zero, q)], 0)
        tops, scores, floored = [], [], True
        for k, v, bias, masked in sources:
            sc = lax.dot_general(k, both, (((1,), (1,)), ((), ())), preferred_element_type=jnp.float32)
            if masked:
                sc = jnp.where(causal, sc, NEG)
            top = jnp.max(sc, 0, keepdims=True)
            if bias is None:
                floored = False
            else:
                top = top + bias
            tops.append(top)
            scores.append(sc)
        high = tops[0]
        for top in tops[1:]:
            high = jnp.maximum(high, top)
        if floored:
            high = jnp.maximum(high, FLOOR)
        total, mixed = None, None
        for (k, v, bias, masked), sc in zip(sources, scores):
            base = high if bias is None else high - bias
            e = jnp.exp2((sc - base) * RATE)
            t = jnp.sum(e, 0, keepdims=True)
            o = lax.dot_general(v, e.astype(jnp.bfloat16), (((0,), (0,)), ((), ())),
                                preferred_element_type=jnp.float32)
            total = t if total is None else total + t
            mixed = o if mixed is None else mixed + o
        return jnp.where(first, mixed[:, :rows], mixed[:, rows:]), high, total

    def merge(items, floored=False):
        high = items[0][1]
        for item in items[1:]:
            high = jnp.maximum(high, item[1])
        if floored:
            high = jnp.maximum(high, FLOOR)
        mixed, total = None, None
        for o, top, t in items:
            w = jnp.exp2((top - high) * RATE)
            mixed = o * spread(w) if mixed is None else mixed + o * spread(w)
            total = t * w if total is None else total + t * w
        return mixed, high, total

    def keep(k, c, p, item):
        o, top, t = item
        part_out[k, c, pl.ds(p * PAIR, PAIR), :] = o.astype(jnp.bfloat16)
        at = 4 * p
        stat_out[k, c, pl.ds(at, 1), :] = top[:, :rows]
        stat_out[k, c, pl.ds(at + 1, 1), :] = top[:, rows:]
        stat_out[k, c, pl.ds(at + 2, 1), :] = t[:, :rows]
        stat_out[k, c, pl.ds(at + 3, 1), :] = t[:, rows:]

    def arrived(r, c, p, bias=None):
        o = part_in[r, c, pl.ds(p * PAIR, PAIR), :].astype(jnp.float32)
        at = 4 * p
        lines = [stat_in[r, c, pl.ds(at + n, 1), :] for n in range(4)]
        top = jnp.concatenate(lines[:2], 1)
        if bias is not None:
            top = top + bias
        return o, top, jnp.concatenate(lines[2:], 1)

    def finish(g, c, p, item):
        o, top, t = item
        o = o * spread(1.0 / t)
        final[g, :, pl.ds(pl.multiple_of(c * wide + p * PAIR, PAIR), PAIR)] = o.T.astype(jnp.bfloat16)

    def mine(a, c, p):
        return piece(own.at[a], c, p)

    def sent(r, c, p):
        return piece(got.at[r], c, p)

    def self_part(g, c, p):
        q, k, v = (mine(3 * g + n, c, p) for n in range(3))
        return attend(q, [(k, v, None, True)])

    def own_bias(slot):
        return flag[pl.ds(slot, 1), :]

    def far_bias(slot):
        return flag_in[pl.ds(slot, 1), :]

    loads = [pltpu.make_async_copy(ins[a].at[0], own.at[a], load_sem.at[a]) for a in range(6)]
    for copy in loads:
        copy.start()
    bias = [jnp.where(kb[0, n] >= 0, 0.0, NEG) for n in range(2)]
    flag_row = lax.broadcasted_iota(jnp.int32, flag.shape, 0)
    flag[...] = jnp.where(flag_row == 0, bias[0], bias[1])

    barrier = pltpu.get_barrier_semaphore()
    for where in (left, right):
        pl.semaphore_signal(barrier, inc=1, device_id=where, device_id_type=MESH)

    @pl.when(s > 0)
    def _():
        pl.semaphore_signal(barrier, inc=1, device_id=below, device_id_type=MESH)

    @pl.when(s < sections - 1)
    def _():
        pl.semaphore_signal(barrier, inc=1, device_id=above, device_id_type=MESH)

    edges = jnp.where(s > 0, 1, 0) + jnp.where(s < sections - 1, 1, 0)
    pl.semaphore_wait(barrier, 2 + edges)

    def flags(k, src, where):
        return remote(src, flag_in, flag_send.at[k], flag_recv.at[0], where)

    def wait_loads():
        for copy in loads:
            copy.wait()

    def ahead(send, count=AHEAD):
        def go(c, carry):
            send(c)
            return carry

        lax.fori_loop(0, min(count, steps), go, 0)

    def run(extra, body):
        def go(t, carry):
            body(t)
            return carry

        lax.fori_loop(0, steps + extra, go, 0)

    def when_chunk(c, act):
        @pl.when(jnp.logical_and(c >= 0, c < steps))
        def _():
            act(c)

    def settle(n_data, n_part):
        def go(c, carry):
            for k in range(n_data):
                data(k, c, got.at[0], 0, right).wait_send()
            for k in range(n_part):
                for copy in parts(k, c, part_out.at[k], stat_out.at[k], 0, right):
                    copy.wait_send()
            return carry

        lax.fori_loop(0, steps, go, 0)

    @pl.when(x == 0)
    def _():
        def send(c):
            send_in(0, c, KD, 0, right)
            send_in(1, c, VD, 1, right)

        ahead(send)
        wait_loads()
        flags(0, flag, right).wait_recv()

        def hub(c):
            wait_data(c, 0, 1, 3, 4)
            for p in range(PAIRS):
                k0, v0 = mine(KU, c, p), mine(VU, c, p)
                k1, v1 = sent(0, c, p), sent(1, c, p)
                keep(1, c, p, attend(sent(3, c, p), [(k1, v1, far_bias(0), False), (k0, v0, far_bias(1), False)]))
            send_part(1, c, 3, left)
            for p in range(PAIRS):
                keep(2, c, p, attend(sent(4, c, p), [(sent(0, c, p), sent(1, c, p), None, False)]))
            send_part(2, c, 2, left)
            for p in range(PAIRS):
                finish(1, c, p, self_part(1, c, p))
                finish(0, c, p, self_part(0, c, p))
            send_out(1, c)
            send_out(0, c)

        def near(c):
            wait_data(c, 2)
            for p in range(PAIRS):
                keep(0, c, p, attend(sent(2, c, p), [(mine(KU, c, p), mine(VU, c, p), None, False)]))
            send_part(0, c, 0, right)

        def body(t):
            when_chunk(t + AHEAD, send)
            when_chunk(t, hub)
            when_chunk(t - SKEW, near)

        run(SKEW, body)
        settle(2, 3)

    @pl.when(x == 1)
    def _():
        def send(c):
            send_in(0, c, KU, 0, left)
            send_in(1, c, VU, 1, left)

        def send_q(c):
            send_in(2, c, QU, 2, left)

        ahead(send)
        ahead(send_q, AHEAD - SKEW)
        wait_loads()
        flags(0, flag, right).wait_recv()

        def hub(c):
            wait_data(c, 0, 1, 2, 3)
            for p in range(PAIRS):
                keep(1, c, p, attend(sent(3, c, p), [(mine(KD, c, p), mine(VD, c, p), None, False)]))
            send_part(1, c, 1, right)
            for p in range(PAIRS):
                k1, v1 = mine(KD, c, p), mine(VD, c, p)
                k0, v0 = sent(0, c, p), sent(1, c, p)
                keep(0, c, p, attend(sent(2, c, p), [(k1, v1, far_bias(0), False), (k0, v0, far_bias(1), False)]))
            send_part(0, c, 0, right)
            for p in range(PAIRS):
                k1, v1 = mine(KD, c, p), mine(VD, c, p)
                k0, v0 = sent(0, c, p), sent(1, c, p)
                finish(0, c, p, attend(mine(QD, c, p), [(k1, v1, None, True), (k0, v0, own_bias(0), False)]))
            send_out(0, c)

        def close(c):
            own_part = [self_part(1, c, p) for p in range(PAIRS)]
            wait_part(c, 0)
            for p in range(PAIRS):
                finish(1, c, p, merge([own_part[p], arrived(0, c, p, own_bias(0))]))
            send_out(1, c)

        def body(t):
            when_chunk(t + AHEAD, send)
            when_chunk(t + AHEAD - SKEW, send_q)
            when_chunk(t, hub)
            when_chunk(t - SKEW - LAG, close)

        run(SKEW + LAG, body)
        settle(3, 2)

    @pl.when(x == 2)
    def _():
        flags(0, flag, left).start()
        flags(1, flag, right).start()

        def send(c):
            send_in(1, c, QU, 0, right)

        def send_q(c):
            send_in(0, c, QD, 2, left)

        ahead(send)
        ahead(send_q, NEAR)

        def relay(c):
            wait_data(c, 0)
            send_on(2, c, 0, 3, left)

        for c in range(min(RELAY, steps)):
            relay(c)
        wait_loads()
        flags(0, flag, right).wait_recv()

        def side(c):
            wait_data(c, 1)
            for p in range(PAIRS):
                keep(1, c, p, attend(sent(1, c, p), [(mine(KU, c, p), mine(VU, c, p), None, False)]))
            send_part(1, c, 1, right)

        def middle(c):
            near = [attend(sent(0, c, p), [(mine(KD, c, p), mine(VD, c, p), far_bias(0), False)])
                    for p in range(PAIRS)]
            wait_part(c, 1)
            for p in range(PAIRS):
                keep(0, c, p, merge([near[p], arrived(1, c, p, far_bias(1))], True))
            send_part(0, c, 0, right)
            own_part = [self_part(0, c, p) for p in range(PAIRS)]
            wait_part(c, 0)
            for p in range(PAIRS):
                finish(0, c, p, merge([own_part[p], arrived(0, c, p)]))
            send_out(0, c)

        def close(c):
            own_part = [self_part(1, c, p) for p in range(PAIRS)]
            wait_part(c, 2)
            for p in range(PAIRS):
                finish(1, c, p, merge([own_part[p], arrived(2, c, p)]))
            send_out(1, c)

        def body(t):
            when_chunk(t + AHEAD, send)
            when_chunk(t + NEAR, send_q)
            when_chunk(t + RELAY, relay)
            when_chunk(t, side)
            when_chunk(t - LAG, middle)
            when_chunk(t - 2 * LAG, close)

        run(2 * LAG, body)
        settle(3, 2)
        for k in range(2):
            flags(k, flag, right).wait_send()

    @pl.when(x == 3)
    def _():
        flags(0, flag, left).start()

        def send(c):
            send_in(0, c, QD, 0, left)
            send_in(1, c, QU, 1, left)

        def send_q(c):
            send_in(2, c, QU, 4, right)

        ahead(send)
        ahead(send_q, NEAR)
        flags(0, flag, right).wait_recv()
        flags(1, flag_in, right).start()

        def relay(c):
            wait_data(c, 0)
            send_on(3, c, 0, 3, right)

        for c in range(min(RELAY, steps)):
            relay(c)
        wait_loads()

        def middle(c):
            wait_part(c, 3)
            relay_part(0, c, 3, 2, left)
            own_part = [self_part(1, c, p) for p in range(PAIRS)]
            wait_part(c, 1, 2)
            for p in range(PAIRS):
                items = [own_part[p], arrived(1, c, p, own_bias(0)), arrived(2, c, p, own_bias(1))]
                finish(1, c, p, merge(items))
            send_out(1, c)

        def close(c):
            own_part = [self_part(0, c, p) for p in range(PAIRS)]
            wait_part(c, 0)
            for p in range(PAIRS):
                finish(0, c, p, merge([own_part[p], arrived(0, c, p)]))
            send_out(0, c)

        def body(t):
            when_chunk(t + AHEAD, send)
            when_chunk(t + NEAR, send_q)
            when_chunk(t + RELAY, relay)
            when_chunk(t - LAG, middle)
            when_chunk(t - 2 * LAG, close)

        run(2 * LAG, body)
        settle(4, 1)
        for k in range(2):
            flags(k, flag, right).wait_send()

    for g in range(2):
        def done(c, carry, g=g):
            @pl.when(ends(g))
            def _():
                out_local(g, c).wait()

            @pl.when(jnp.logical_not(ends(g)))
            def _():
                out_remote(g, c).wait_send()

            @pl.when(jnp.logical_not(ends(1 - g)))
            def _():
                out_remote(g, c).wait_recv()

            return carry

        lax.fori_loop(0, steps, done, 0)


def solution(mesh):
    sections, spacing = mesh.shape["section"], mesh.shape["ctx"] // 4

    def on_device(dq, dk, dv, uq, uk, uv, key_blocks):
        _, rows, width = dq.shape
        wide = PAIRS * PAIR
        steps = width // wide
        half, full = jnp.bfloat16, jnp.float32
        dma = pltpu.SemaphoreType.DMA
        whole = pl.BlockSpec(memory_space=pl.ANY)
        out = jax.ShapeDtypeStruct(dq.shape, half)

        def body(*refs):
            kernel(sections, spacing, *refs)

        return pl.pallas_call(
            body,
            out_shape=(out, out),
            in_specs=[pl.BlockSpec(memory_space=pltpu.SMEM)] + [whole] * 6,
            out_specs=(whole, whole),
            scratch_shapes=[
                pltpu.VMEM((6, rows, width), half),
                pltpu.VMEM((5, rows, width), half),
                pltpu.VMEM((4, steps, wide, rows), half),
                pltpu.VMEM((4, steps, 4 * PAIRS, rows), full),
                pltpu.VMEM((3, steps, wide, rows), half),
                pltpu.VMEM((3, steps, 4 * PAIRS, rows), full),
                pltpu.VMEM((2, rows, width), half),
                pltpu.VMEM((8, 2 * rows), full),
                pltpu.VMEM((8, 2 * rows), full),
                dma((6,)),
                dma((4, steps)),
                dma((5, steps)),
                dma((3, steps)),
                dma((4, steps)),
                dma((3, steps)),
                dma((4, steps)),
                dma((2, steps)),
                dma((2, steps)),
                dma((2,)),
                dma((1,)),
            ],
            compiler_params=pltpu.CompilerParams(
                collective_id=0, has_side_effects=True, vmem_limit_bytes=67043328),
        )(key_blocks, dq, dk, dv, uq, uk, uv)

    placed = (P("section", "ctx", None),) * 6 + (P("ctx", None),)
    return jax.shard_map(
        on_device,
        mesh=mesh,
        in_specs=placed,
        out_specs=(P("section", "ctx", None), P("section", "ctx", None)),
        check_vma=False,
    )
```

```python
import math

import jax
import jax.numpy as jnp
from jax import lax
from jax.experimental import pallas as pl
from jax.experimental.pallas import tpu as pltpu
from jax.sharding import PartitionSpec as P

HEAD_DIM = 64
PAIR = 2 * HEAD_DIM
PAIRS = 1
DEEP = 10
AHEAD = 6
NEAR = 4
RAMP = 5
LAG = 2
FAR = 5
SKEW = 2
NEG = -1e30
FLOOR = -5e29
RATE = math.log2(math.e) / math.sqrt(HEAD_DIM)
MESH = pl.DeviceIdType.MESH


def kernel(sections, spacing, kb, dq, dk, dv, uq, uk, uv, fwd, hand, own, got, part_in, stat_in,
           part_out, stat_out, final, flag, flag_in, load_sem, data_send, data_recv, part_send,
           part_recv, stat_send, stat_recv, out_send, out_recv, flag_send, flag_recv):
    s = lax.axis_index("section")
    i = lax.axis_index("ctx")
    x = i // spacing
    rest = i - x * spacing
    right = (s, lax.rem(x + 1, 4) * spacing + rest)
    left = (s, lax.rem(x + 3, 4) * spacing + rest)
    below = (lax.max(s - 1, 0), i)
    above = (lax.min(s + 1, sections - 1), i)
    rows = own.shape[1]
    wide = PAIRS * PAIR
    steps = own.shape[2] // wide
    ins = (dq, dk, dv, uq, uk, uv)
    QD, KD, VD, QU, KU, VU = range(6)

    def lanes(c):
        return pl.ds(pl.multiple_of(c * wide, wide), wide)

    def remote(src, dst, send, recv, where):
        return pltpu.make_async_remote_copy(
            src_ref=src, dst_ref=dst, send_sem=send, recv_sem=recv, device_id=where,
            device_id_type=MESH)

    def data(k, c, src, r, where):
        return remote(src.at[:, lanes(c)], got.at[r, :, lanes(c)], data_send.at[k, c],
                      data_recv.at[r, c], where)

    def send_in(k, c, a, r, where):
        data(k, c, ins[a].at[0], r, where).start()

    def send_on(k, c, r0, r, where):
        data(k, c, got.at[r0], r, where).start()

    def wait_data(c, *slots):
        for r in slots:
            data(0, c, got.at[r], r, right).wait_recv()

    def parts(k, c, src, stat, r, where):
        return (remote(src.at[c], part_in.at[r, c], part_send.at[k, c], part_recv.at[r, c], where),
                remote(stat.at[c], stat_in.at[r, c], stat_send.at[k, c], stat_recv.at[r, c], where))

    def send_part(k, c, r, where):
        for copy in parts(k, c, part_out.at[k], stat_out.at[k], r, where):
            copy.start()

    def relay_part(k, c, r0, r, where):
        for copy in parts(k, c, part_in.at[r0], stat_in.at[r0], r, where):
            copy.start()

    def wait_part(c, *slots):
        for r in slots:
            for copy in parts(0, c, part_in.at[r], stat_in.at[r], r, right):
                copy.wait_recv()

    def out_remote(g, c):
        src = final.at[g, :, lanes(c)]
        dst = (fwd, hand)[g].at[0, :, lanes(c)]
        return remote(src, dst, out_send.at[g, c], out_recv.at[g, c], (above, below)[g])

    def out_local(g, c):
        dst = (hand, fwd)[g].at[0, :, lanes(c)]
        return pltpu.make_async_copy(final.at[g, :, lanes(c)], dst, out_send.at[g, c])

    def ends(g):
        return s == (sections - 1, 0)[g]

    def send_out(g, c):
        @pl.when(ends(g))
        def _():
            out_local(g, c).start()

        @pl.when(jnp.logical_not(ends(g)))
        def _():
            out_remote(g, c).start()

    lane = lax.broadcasted_iota(jnp.int32, (rows, PAIR), 1)
    row = lax.broadcasted_iota(jnp.int32, (PAIR, rows), 0)
    first = row < HEAD_DIM
    key = lax.broadcasted_iota(jnp.int32, (rows, 2 * rows), 0)
    query = lax.broadcasted_iota(jnp.int32, (rows, 2 * rows), 1)
    causal = key <= lax.rem(query, rows)

    def piece(ref, c, p):
        return ref[:, pl.ds(pl.multiple_of(c * wide + p * PAIR, PAIR), PAIR)]

    def spread(v):
        return jnp.where(first, v[:, :rows], v[:, rows:])

    def attend(q, sources):
        zero = jnp.zeros_like(q)
        both = jnp.concatenate([jnp.where(lane < HEAD_DIM, q, zero), jnp.where(lane < HEAD_DIM, zero, q)], 0)
        tops, scores, floored = [], [], True
        for k, v, bias, masked in sources:
            sc = lax.dot_general(k, both, (((1,), (1,)), ((), ())), preferred_element_type=jnp.float32)
            if masked:
                sc = jnp.where(causal, sc, NEG)
            top = jnp.max(sc, 0, keepdims=True)
            if bias is None:
                floored = False
            else:
                top = top + bias
            tops.append(top)
            scores.append(sc)
        high = tops[0]
        for top in tops[1:]:
            high = jnp.maximum(high, top)
        if floored:
            high = jnp.maximum(high, FLOOR)
        total, mixed = None, None
        for (k, v, bias, masked), sc in zip(sources, scores):
            base = high if bias is None else high - bias
            e = jnp.exp2((sc - base) * RATE)
            t = jnp.sum(e, 0, keepdims=True)
            o = lax.dot_general(v, e.astype(jnp.bfloat16), (((0,), (0,)), ((), ())),
                                preferred_element_type=jnp.float32)
            total = t if total is None else total + t
            mixed = o if mixed is None else mixed + o
        return jnp.where(first, mixed[:, :rows], mixed[:, rows:]), high, total

    def merge(items, floored=False):
        high = items[0][1]
        for item in items[1:]:
            high = jnp.maximum(high, item[1])
        if floored:
            high = jnp.maximum(high, FLOOR)
        mixed, total = None, None
        for o, top, t in items:
            w = jnp.exp2((top - high) * RATE)
            mixed = o * spread(w) if mixed is None else mixed + o * spread(w)
            total = t * w if total is None else total + t * w
        return mixed, high, total

    def keep(k, c, p, item):
        o, top, t = item
        part_out[k, c, pl.ds(p * PAIR, PAIR), :] = o.astype(jnp.bfloat16)
        at = 4 * p
        stat_out[k, c, pl.ds(at, 1), :] = top[:, :rows]
        stat_out[k, c, pl.ds(at + 1, 1), :] = top[:, rows:]
        stat_out[k, c, pl.ds(at + 2, 1), :] = t[:, :rows]
        stat_out[k, c, pl.ds(at + 3, 1), :] = t[:, rows:]

    def arrived(r, c, p, bias=None):
        o = part_in[r, c, pl.ds(p * PAIR, PAIR), :].astype(jnp.float32)
        at = 4 * p
        lines = [stat_in[r, c, pl.ds(at + n, 1), :] for n in range(4)]
        top = jnp.concatenate(lines[:2], 1)
        if bias is not None:
            top = top + bias
        return o, top, jnp.concatenate(lines[2:], 1)

    def finish(g, c, p, item):
        o, top, t = item
        o = o * spread(1.0 / t)
        final[g, :, pl.ds(pl.multiple_of(c * wide + p * PAIR, PAIR), PAIR)] = o.T.astype(jnp.bfloat16)

    def mine(a, c, p):
        return piece(own.at[a], c, p)

    def sent(r, c, p):
        return piece(got.at[r], c, p)

    def self_part(g, c, p):
        q, k, v = (mine(3 * g + n, c, p) for n in range(3))
        return attend(q, [(k, v, None, True)])

    def own_bias(slot):
        return flag[pl.ds(slot, 1), :]

    def far_bias(slot):
        return flag_in[pl.ds(slot, 1), :]

    loads = [pltpu.make_async_copy(ins[a].at[0], own.at[a], load_sem.at[a]) for a in range(6)]
    for copy in loads:
        copy.start()
    bias = [jnp.where(kb[0, n] >= 0, 0.0, NEG) for n in range(2)]
    flag_row = lax.broadcasted_iota(jnp.int32, flag.shape, 0)
    flag[...] = jnp.where(flag_row == 0, bias[0], bias[1])

    barrier = pltpu.get_barrier_semaphore()
    for where in (left, right):
        pl.semaphore_signal(barrier, inc=1, device_id=where, device_id_type=MESH)

    @pl.when(s > 0)
    def _():
        pl.semaphore_signal(barrier, inc=1, device_id=below, device_id_type=MESH)

    @pl.when(s < sections - 1)
    def _():
        pl.semaphore_signal(barrier, inc=1, device_id=above, device_id_type=MESH)

    edges = jnp.where(s > 0, 1, 0) + jnp.where(s < sections - 1, 1, 0)
    pl.semaphore_wait(barrier, 2 + edges)

    def flags(k, src, where):
        return remote(src, flag_in, flag_send.at[k], flag_recv.at[0], where)

    def wait_loads():
        for copy in loads:
            copy.wait()

    def ahead(send, count=AHEAD):
        def go(c, carry):
            send(c)
            return carry

        lax.fori_loop(0, min(count, steps), go, 0)

    def run(extra, body):
        def go(t, carry):
            body(t)
            return carry

        lax.fori_loop(0, steps + extra, go, 0)

    def when_chunk(c, act):
        @pl.when(jnp.logical_and(c >= 0, c < steps))
        def _():
            act(c)

    def ramp(t, relay):
        early = jnp.asarray(t < RAMP)
        when_chunk(jnp.where(early, 2 * t + 2, t + RAMP + 2), relay)
        when_chunk(jnp.where(early, 2 * t + 3, -1), relay)

    def settle(n_data, n_part):
        def go(c, carry):
            for k in range(n_data):
                data(k, c, got.at[0], 0, right).wait_send()
            for k in range(n_part):
                for copy in parts(k, c, part_out.at[k], stat_out.at[k], 0, right):
                    copy.wait_send()
            return carry

        lax.fori_loop(0, steps, go, 0)

    @pl.when(x == 0)
    def _():
        def send(c):
            send_in(0, c, KD, 0, right)
            send_in(1, c, VD, 1, right)

        ahead(send)
        wait_loads()
        flags(0, flag, right).wait_recv()

        def hub(c):
            wait_data(c, 0, 1, 3, 4)
            for p in range(PAIRS):
                k0, v0 = mine(KU, c, p), mine(VU, c, p)
                k1, v1 = sent(0, c, p), sent(1, c, p)
                keep(1, c, p, attend(sent(3, c, p), [(k1, v1, far_bias(0), False), (k0, v0, far_bias(1), False)]))
            send_part(1, c, 3, left)
            for p in range(PAIRS):
                keep(2, c, p, attend(sent(4, c, p), [(sent(0, c, p), sent(1, c, p), None, False)]))
            send_part(2, c, 2, left)
            for p in range(PAIRS):
                finish(1, c, p, self_part(1, c, p))
                finish(0, c, p, self_part(0, c, p))
            send_out(1, c)
            send_out(0, c)

        def near(c):
            wait_data(c, 2)
            for p in range(PAIRS):
                keep(0, c, p, attend(sent(2, c, p), [(mine(KU, c, p), mine(VU, c, p), None, False)]))
            send_part(0, c, 0, right)

        def body(t):
            when_chunk(t + AHEAD, send)
            when_chunk(t, hub)
            when_chunk(t - SKEW, near)

        run(SKEW, body)
        settle(2, 3)

    @pl.when(x == 1)
    def _():
        def send(c):
            send_in(0, c, KU, 0, left)
            send_in(1, c, VU, 1, left)

        def send_q(c):
            send_in(2, c, QU, 2, left)

        def send_all(c):
            when_chunk(c, send)
            when_chunk(c - SKEW, send_q)

        ahead(send_all, DEEP)
        wait_loads()
        flags(0, flag, right).wait_recv()

        def hub(c):
            wait_data(c, 0, 1, 2, 3)
            for p in range(PAIRS):
                keep(1, c, p, attend(sent(3, c, p), [(mine(KD, c, p), mine(VD, c, p), None, False)]))
            send_part(1, c, 1, right)
            for p in range(PAIRS):
                k1, v1 = mine(KD, c, p), mine(VD, c, p)
                k0, v0 = sent(0, c, p), sent(1, c, p)
                keep(0, c, p, attend(sent(2, c, p), [(k1, v1, far_bias(0), False), (k0, v0, far_bias(1), False)]))
            send_part(0, c, 0, right)
            for p in range(PAIRS):
                k1, v1 = mine(KD, c, p), mine(VD, c, p)
                k0, v0 = sent(0, c, p), sent(1, c, p)
                finish(0, c, p, attend(mine(QD, c, p), [(k1, v1, None, True), (k0, v0, own_bias(0), False)]))
            send_out(0, c)

        def close(c):
            own_part = [self_part(1, c, p) for p in range(PAIRS)]
            wait_part(c, 0)
            for p in range(PAIRS):
                finish(1, c, p, merge([own_part[p], arrived(0, c, p, own_bias(0))]))
            send_out(1, c)

        def body(t):
            send_all(t + DEEP)
            when_chunk(t, hub)
            when_chunk(t - SKEW - LAG, close)

        run(SKEW + LAG, body)
        settle(3, 2)

    @pl.when(x == 2)
    def _():
        flags(0, flag, left).start()
        flags(1, flag, right).start()

        def send(c):
            send_in(1, c, QU, 0, right)

        def send_q(c):
            send_in(0, c, QD, 2, left)

        ahead(send_q, NEAR)
        ahead(send, DEEP)

        def relay(c):
            wait_data(c, 0)
            send_on(2, c, 0, 3, left)

        ramp(-1, relay)
        wait_loads()
        flags(0, flag, right).wait_recv()

        def side(c):
            wait_data(c, 1)
            for p in range(PAIRS):
                keep(1, c, p, attend(sent(1, c, p), [(mine(KU, c, p), mine(VU, c, p), None, False)]))
            send_part(1, c, 1, right)

        def middle(c):
            near = [attend(sent(0, c, p), [(mine(KD, c, p), mine(VD, c, p), far_bias(0), False)])
                    for p in range(PAIRS)]
            wait_part(c, 1)
            for p in range(PAIRS):
                keep(0, c, p, merge([near[p], arrived(1, c, p, far_bias(1))], True))
            send_part(0, c, 0, right)
            own_part = [self_part(0, c, p) for p in range(PAIRS)]
            wait_part(c, 0)
            for p in range(PAIRS):
                finish(0, c, p, merge([own_part[p], arrived(0, c, p)]))
            send_out(0, c)

        def close(c):
            own_part = [self_part(1, c, p) for p in range(PAIRS)]
            wait_part(c, 2)
            for p in range(PAIRS):
                finish(1, c, p, merge([own_part[p], arrived(2, c, p)]))
            send_out(1, c)

        def body(t):
            when_chunk(t + DEEP, send)
            when_chunk(t + NEAR, send_q)
            ramp(t, relay)
            when_chunk(t, side)
            when_chunk(t - LAG, middle)
            when_chunk(t - FAR, close)

        run(FAR, body)
        settle(3, 2)
        for k in range(2):
            flags(k, flag, right).wait_send()

    @pl.when(x == 3)
    def _():
        flags(0, flag, left).start()

        def send(c):
            send_in(0, c, QD, 0, left)

        def send_q(c):
            send_in(1, c, QU, 1, left)
            send_in(2, c, QU, 4, right)

        def first_sends(c):
            send(c)
            when_chunk(jnp.where(c < NEAR, c, -1), send_q)

        ahead(first_sends, DEEP)
        flags(0, flag, right).wait_recv()
        flags(1, flag_in, right).start()

        def relay(c):
            wait_data(c, 0)
            send_on(3, c, 0, 3, right)

        ramp(-1, relay)
        wait_loads()

        def middle(c):
            wait_part(c, 3)
            relay_part(0, c, 3, 2, left)
            own_part = [self_part(1, c, p) for p in range(PAIRS)]
            wait_part(c, 1, 2)
            for p in range(PAIRS):
                items = [own_part[p], arrived(1, c, p, own_bias(0)), arrived(2, c, p, own_bias(1))]
                finish(1, c, p, merge(items))
            send_out(1, c)

        def close(c):
            own_part = [self_part(0, c, p) for p in range(PAIRS)]
            wait_part(c, 0)
            for p in range(PAIRS):
                finish(0, c, p, merge([own_part[p], arrived(0, c, p)]))
            send_out(0, c)

        def body(t):
            when_chunk(t + DEEP, send)
            when_chunk(t + NEAR, send_q)
            ramp(t, relay)
            when_chunk(t - LAG, middle)
            when_chunk(t - FAR, close)

        run(FAR, body)
        settle(4, 1)
        for k in range(2):
            flags(k, flag, right).wait_send()

    for g in range(2):
        def done(c, carry, g=g):
            @pl.when(ends(g))
            def _():
                out_local(g, c).wait()

            @pl.when(jnp.logical_not(ends(g)))
            def _():
                out_remote(g, c).wait_send()

            @pl.when(jnp.logical_not(ends(1 - g)))
            def _():
                out_remote(g, c).wait_recv()

            return carry

        lax.fori_loop(0, steps, done, 0)


def solution(mesh):
    sections, spacing = mesh.shape["section"], mesh.shape["ctx"] // 4

    def on_device(dq, dk, dv, uq, uk, uv, key_blocks):
        _, rows, width = dq.shape
        wide = PAIRS * PAIR
        steps = width // wide
        half, full = jnp.bfloat16, jnp.float32
        dma = pltpu.SemaphoreType.DMA
        whole = pl.BlockSpec(memory_space=pl.ANY)
        out = jax.ShapeDtypeStruct(dq.shape, half)

        def body(*refs):
            kernel(sections, spacing, *refs)

        return pl.pallas_call(
            body,
            out_shape=(out, out),
            in_specs=[pl.BlockSpec(memory_space=pltpu.SMEM)] + [whole] * 6,
            out_specs=(whole, whole),
            scratch_shapes=[
                pltpu.VMEM((6, rows, width), half),
                pltpu.VMEM((5, rows, width), half),
                pltpu.VMEM((4, steps, wide, rows), half),
                pltpu.VMEM((4, steps, 4 * PAIRS, rows), full),
                pltpu.VMEM((3, steps, wide, rows), half),
                pltpu.VMEM((3, steps, 4 * PAIRS, rows), full),
                pltpu.VMEM((2, rows, width), half),
                pltpu.VMEM((8, 2 * rows), full),
                pltpu.VMEM((8, 2 * rows), full),
                dma((6,)),
                dma((4, steps)),
                dma((5, steps)),
                dma((3, steps)),
                dma((4, steps)),
                dma((3, steps)),
                dma((4, steps)),
                dma((2, steps)),
                dma((2, steps)),
                dma((2,)),
                dma((1,)),
            ],
            compiler_params=pltpu.CompilerParams(
                collective_id=0, has_side_effects=True, vmem_limit_bytes=67043328),
        )(key_blocks, dq, dk, dv, uq, uk, uv)

    placed = (P("section", "ctx", None),) * 6 + (P("ctx", None),)
    return jax.shard_map(
        on_device,
        mesh=mesh,
        in_specs=placed,
        out_specs=(P("section", "ctx", None), P("section", "ctx", None)),
        check_vma=False,
    )
```

```python
import math

import jax
import jax.numpy as jnp
from jax import lax
from jax.experimental import pallas as pl
from jax.experimental.pallas import tpu as pltpu
from jax.sharding import PartitionSpec as P

HEAD_DIM = 64
PAIR = 2 * HEAD_DIM
PAIRS = 1
AHEAD = 8
NEAR = 4
RELAY = 4
LAG = 3
SKEW = 3
NEG = -1e30
FLOOR = -5e29
RATE = math.log2(math.e) / math.sqrt(HEAD_DIM)
MESH = pl.DeviceIdType.MESH


def kernel(sections, spacing, kb, dq, dk, dv, uq, uk, uv, fwd, hand, own, got, part_in, stat_in,
           part_out, stat_out, final, flag, flag_in, load_sem, data_send, data_recv, part_send,
           part_recv, stat_send, stat_recv, out_send, out_recv, flag_send, flag_recv):
    s = lax.axis_index("section")
    i = lax.axis_index("ctx")
    x = i // spacing
    rest = i - x * spacing
    right = (s, lax.rem(x + 1, 4) * spacing + rest)
    left = (s, lax.rem(x + 3, 4) * spacing + rest)
    below = (lax.max(s - 1, 0), i)
    above = (lax.min(s + 1, sections - 1), i)
    rows = own.shape[1]
    wide = PAIRS * PAIR
    steps = own.shape[2] // wide
    ins = (dq, dk, dv, uq, uk, uv)
    QD, KD, VD, QU, KU, VU = range(6)

    def lanes(c):
        return pl.ds(pl.multiple_of(c * wide, wide), wide)

    def remote(src, dst, send, recv, where):
        return pltpu.make_async_remote_copy(
            src_ref=src, dst_ref=dst, send_sem=send, recv_sem=recv, device_id=where,
            device_id_type=MESH)

    def data(k, c, src, r, where):
        return remote(src.at[:, lanes(c)], got.at[r, :, lanes(c)], data_send.at[k, c],
                      data_recv.at[r, c], where)

    def send_in(k, c, a, r, where):
        data(k, c, ins[a].at[0], r, where).start()

    def send_on(k, c, r0, r, where):
        data(k, c, got.at[r0], r, where).start()

    def wait_data(c, *slots):
        for r in slots:
            data(0, c, got.at[r], r, right).wait_recv()

    def parts(k, c, src, stat, r, where):
        return (remote(src.at[c], part_in.at[r, c], part_send.at[k, c], part_recv.at[r, c], where),
                remote(stat.at[c], stat_in.at[r, c], stat_send.at[k, c], stat_recv.at[r, c], where))

    def send_part(k, c, r, where):
        for copy in parts(k, c, part_out.at[k], stat_out.at[k], r, where):
            copy.start()

    def relay_part(k, c, r0, r, where):
        for copy in parts(k, c, part_in.at[r0], stat_in.at[r0], r, where):
            copy.start()

    def wait_part(c, *slots):
        for r in slots:
            for copy in parts(0, c, part_in.at[r], stat_in.at[r], r, right):
                copy.wait_recv()

    def out_remote(g, c):
        src = final.at[g, :, lanes(c)]
        dst = (fwd, hand)[g].at[0, :, lanes(c)]
        return remote(src, dst, out_send.at[g, c], out_recv.at[g, c], (above, below)[g])

    def out_local(g, c):
        dst = (hand, fwd)[g].at[0, :, lanes(c)]
        return pltpu.make_async_copy(final.at[g, :, lanes(c)], dst, out_send.at[g, c])

    def ends(g):
        return s == (sections - 1, 0)[g]

    def send_out(g, c):
        @pl.when(ends(g))
        def _():
            out_local(g, c).start()

        @pl.when(jnp.logical_not(ends(g)))
        def _():
            out_remote(g, c).start()

    lane = lax.broadcasted_iota(jnp.int32, (rows, PAIR), 1)
    row = lax.broadcasted_iota(jnp.int32, (PAIR, rows), 0)
    first = row < HEAD_DIM
    key = lax.broadcasted_iota(jnp.int32, (rows, 2 * rows), 0)
    query = lax.broadcasted_iota(jnp.int32, (rows, 2 * rows), 1)
    causal = key <= lax.rem(query, rows)

    def piece(ref, c, p):
        return ref[:, pl.ds(pl.multiple_of(c * wide + p * PAIR, PAIR), PAIR)]

    def spread(v):
        return jnp.where(first, v[:, :rows], v[:, rows:])

    def attend(q, sources):
        zero = jnp.zeros_like(q)
        both = jnp.concatenate([jnp.where(lane < HEAD_DIM, q, zero), jnp.where(lane < HEAD_DIM, zero, q)], 0)
        tops, scores, floored = [], [], True
        for k, v, bias, masked in sources:
            sc = lax.dot_general(k, both, (((1,), (1,)), ((), ())), preferred_element_type=jnp.float32)
            if masked:
                sc = jnp.where(causal, sc, NEG)
            top = jnp.max(sc, 0, keepdims=True)
            if bias is None:
                floored = False
            else:
                top = top + bias
            tops.append(top)
            scores.append(sc)
        high = tops[0]
        for top in tops[1:]:
            high = jnp.maximum(high, top)
        if floored:
            high = jnp.maximum(high, FLOOR)
        total, mixed = None, None
        for (k, v, bias, masked), sc in zip(sources, scores):
            base = high if bias is None else high - bias
            e = jnp.exp2((sc - base) * RATE)
            t = jnp.sum(e, 0, keepdims=True)
            o = lax.dot_general(v, e.astype(jnp.bfloat16), (((0,), (0,)), ((), ())),
                                preferred_element_type=jnp.float32)
            total = t if total is None else total + t
            mixed = o if mixed is None else mixed + o
        return jnp.where(first, mixed[:, :rows], mixed[:, rows:]), high, total

    def merge(items, floored=False):
        high = items[0][1]
        for item in items[1:]:
            high = jnp.maximum(high, item[1])
        if floored:
            high = jnp.maximum(high, FLOOR)
        mixed, total = None, None
        for o, top, t in items:
            w = jnp.exp2((top - high) * RATE)
            mixed = o * spread(w) if mixed is None else mixed + o * spread(w)
            total = t * w if total is None else total + t * w
        return mixed, high, total

    def keep(k, c, p, item):
        o, top, t = item
        part_out[k, c, pl.ds(p * PAIR, PAIR), :] = o.astype(jnp.bfloat16)
        at = 4 * p
        stat_out[k, c, pl.ds(at, 1), :] = top[:, :rows]
        stat_out[k, c, pl.ds(at + 1, 1), :] = top[:, rows:]
        stat_out[k, c, pl.ds(at + 2, 1), :] = t[:, :rows]
        stat_out[k, c, pl.ds(at + 3, 1), :] = t[:, rows:]

    def arrived(r, c, p, bias=None):
        o = part_in[r, c, pl.ds(p * PAIR, PAIR), :].astype(jnp.float32)
        at = 4 * p
        lines = [stat_in[r, c, pl.ds(at + n, 1), :] for n in range(4)]
        top = jnp.concatenate(lines[:2], 1)
        if bias is not None:
            top = top + bias
        return o, top, jnp.concatenate(lines[2:], 1)

    def finish(g, c, p, item):
        o, top, t = item
        o = o * spread(1.0 / t)
        final[g, :, pl.ds(pl.multiple_of(c * wide + p * PAIR, PAIR), PAIR)] = o.T.astype(jnp.bfloat16)

    def mine(a, c, p):
        return piece(own.at[a], c, p)

    def sent(r, c, p):
        return piece(got.at[r], c, p)

    def self_part(g, c, p):
        q, k, v = (mine(3 * g + n, c, p) for n in range(3))
        return attend(q, [(k, v, None, True)])

    def own_bias(slot):
        return flag[pl.ds(slot, 1), :]

    def far_bias(slot):
        return flag_in[pl.ds(slot, 1), :]

    loads = [pltpu.make_async_copy(ins[a].at[0], own.at[a], load_sem.at[a]) for a in range(6)]
    for copy in loads:
        copy.start()
    bias = [jnp.where(kb[0, n] >= 0, 0.0, NEG) for n in range(2)]
    flag_row = lax.broadcasted_iota(jnp.int32, flag.shape, 0)
    flag[...] = jnp.where(flag_row == 0, bias[0], bias[1])

    barrier = pltpu.get_barrier_semaphore()
    for where in (left, right):
        pl.semaphore_signal(barrier, inc=1, device_id=where, device_id_type=MESH)

    @pl.when(s > 0)
    def _():
        pl.semaphore_signal(barrier, inc=1, device_id=below, device_id_type=MESH)

    @pl.when(s < sections - 1)
    def _():
        pl.semaphore_signal(barrier, inc=1, device_id=above, device_id_type=MESH)

    edges = jnp.where(s > 0, 1, 0) + jnp.where(s < sections - 1, 1, 0)
    pl.semaphore_wait(barrier, 2 + edges)

    def flags(k, src, where):
        return remote(src, flag_in, flag_send.at[k], flag_recv.at[0], where)

    def wait_loads():
        for copy in loads:
            copy.wait()

    def ahead(send, count=AHEAD):
        def go(c, carry):
            send(c)
            return carry

        lax.fori_loop(0, min(count, steps), go, 0)

    def run(extra, body):
        def go(t, carry):
            body(t)
            return carry

        lax.fori_loop(0, steps + extra, go, 0)

    def when_chunk(c, act):
        @pl.when(jnp.logical_and(c >= 0, c < steps))
        def _():
            act(c)

    def settle(n_data, n_part):
        def go(c, carry):
            for k in range(n_data):
                data(k, c, got.at[0], 0, right).wait_send()
            for k in range(n_part):
                for copy in parts(k, c, part_out.at[k], stat_out.at[k], 0, right):
                    copy.wait_send()
            return carry

        lax.fori_loop(0, steps, go, 0)

    @pl.when(x == 0)
    def _():
        def send(c):
            send_in(0, c, KD, 0, right)
            send_in(1, c, VD, 1, right)

        ahead(send)
        wait_loads()
        flags(0, flag, right).wait_recv()

        def hub(c):
            wait_data(c, 0, 1, 3, 4)
            for p in range(PAIRS):
                k0, v0 = mine(KU, c, p), mine(VU, c, p)
                k1, v1 = sent(0, c, p), sent(1, c, p)
                keep(1, c, p, attend(sent(3, c, p), [(k1, v1, far_bias(0), False), (k0, v0, far_bias(1), False)]))
            send_part(1, c, 3, left)
            for p in range(PAIRS):
                keep(2, c, p, attend(sent(4, c, p), [(sent(0, c, p), sent(1, c, p), None, False)]))
            send_part(2, c, 2, left)
            for p in range(PAIRS):
                finish(1, c, p, self_part(1, c, p))
                finish(0, c, p, self_part(0, c, p))
            send_out(1, c)
            send_out(0, c)

        def near(c):
            wait_data(c, 2)
            for p in range(PAIRS):
                keep(0, c, p, attend(sent(2, c, p), [(mine(KU, c, p), mine(VU, c, p), None, False)]))
            send_part(0, c, 0, right)

        def body(t):
            when_chunk(t + AHEAD, send)
            when_chunk(t, hub)
            when_chunk(t - SKEW, near)

        run(SKEW, body)
        settle(2, 3)

    @pl.when(x == 1)
    def _():
        def send(c):
            send_in(0, c, KU, 0, left)
            send_in(1, c, VU, 1, left)

        def send_q(c):
            send_in(2, c, QU, 2, left)

        ahead(send)
        ahead(send_q, AHEAD - SKEW)
        wait_loads()
        flags(0, flag, right).wait_recv()

        def hub(c):
            wait_data(c, 0, 1, 2, 3)
            for p in range(PAIRS):
                keep(1, c, p, attend(sent(3, c, p), [(mine(KD, c, p), mine(VD, c, p), None, False)]))
            send_part(1, c, 1, right)
            for p in range(PAIRS):
                k1, v1 = mine(KD, c, p), mine(VD, c, p)
                k0, v0 = sent(0, c, p), sent(1, c, p)
                keep(0, c, p, attend(sent(2, c, p), [(k1, v1, far_bias(0), False), (k0, v0, far_bias(1), False)]))
            send_part(0, c, 0, right)
            for p in range(PAIRS):
                k1, v1 = mine(KD, c, p), mine(VD, c, p)
                k0, v0 = sent(0, c, p), sent(1, c, p)
                finish(0, c, p, attend(mine(QD, c, p), [(k1, v1, None, True), (k0, v0, own_bias(0), False)]))
            send_out(0, c)

        def close(c):
            own_part = [self_part(1, c, p) for p in range(PAIRS)]
            wait_part(c, 0)
            for p in range(PAIRS):
                finish(1, c, p, merge([own_part[p], arrived(0, c, p, own_bias(0))]))
            send_out(1, c)

        def body(t):
            when_chunk(t + AHEAD, send)
            when_chunk(t + AHEAD - SKEW, send_q)
            when_chunk(t, hub)
            when_chunk(t - SKEW - 2, close)

        run(SKEW + 2, body)
        settle(3, 2)

    @pl.when(x == 2)
    def _():
        flags(0, flag, left).start()
        flags(1, flag, right).start()

        def send(c):
            send_in(1, c, QU, 0, right)

        def send_q(c):
            send_in(0, c, QD, 2, left)

        ahead(send)
        ahead(send_q, NEAR)

        def relay(c):
            wait_data(c, 0)
            send_on(2, c, 0, 3, left)

        for c in range(min(RELAY, steps)):
            relay(c)
        wait_loads()
        flags(0, flag, right).wait_recv()

        def side(c):
            wait_data(c, 1)
            for p in range(PAIRS):
                keep(1, c, p, attend(sent(1, c, p), [(mine(KU, c, p), mine(VU, c, p), None, False)]))
            send_part(1, c, 1, right)

        def middle(c):
            near = [attend(sent(0, c, p), [(mine(KD, c, p), mine(VD, c, p), far_bias(0), False)])
                    for p in range(PAIRS)]
            wait_part(c, 1)
            for p in range(PAIRS):
                keep(0, c, p, merge([near[p], arrived(1, c, p, far_bias(1))], True))
            send_part(0, c, 0, right)
            own_part = [self_part(0, c, p) for p in range(PAIRS)]
            wait_part(c, 0)
            for p in range(PAIRS):
                finish(0, c, p, merge([own_part[p], arrived(0, c, p)]))
            send_out(0, c)

        def close(c):
            own_part = [self_part(1, c, p) for p in range(PAIRS)]
            wait_part(c, 2)
            for p in range(PAIRS):
                finish(1, c, p, merge([own_part[p], arrived(2, c, p)]))
            send_out(1, c)

        def body(t):
            when_chunk(t + AHEAD, send)
            when_chunk(t + NEAR, send_q)
            when_chunk(t + RELAY, relay)
            when_chunk(t, side)
            when_chunk(t - LAG, middle)
            when_chunk(t - 2 * LAG, close)

        run(2 * LAG, body)
        settle(3, 2)
        for k in range(2):
            flags(k, flag, right).wait_send()

    @pl.when(x == 3)
    def _():
        flags(0, flag, left).start()

        def send(c):
            send_in(0, c, QD, 0, left)
            send_in(1, c, QU, 1, left)

        def send_q(c):
            send_in(2, c, QU, 4, right)

        ahead(send)
        ahead(send_q, NEAR)
        flags(0, flag, right).wait_recv()
        flags(1, flag_in, right).start()

        def relay(c):
            wait_data(c, 0)
            send_on(3, c, 0, 3, right)

        for c in range(min(RELAY, steps)):
            relay(c)
        wait_loads()

        def middle(c):
            wait_part(c, 3)
            relay_part(0, c, 3, 2, left)
            own_part = [self_part(1, c, p) for p in range(PAIRS)]
            wait_part(c, 1, 2)
            for p in range(PAIRS):
                items = [own_part[p], arrived(1, c, p, own_bias(0)), arrived(2, c, p, own_bias(1))]
                finish(1, c, p, merge(items))
            send_out(1, c)

        def close(c):
            own_part = [self_part(0, c, p) for p in range(PAIRS)]
            wait_part(c, 0)
            for p in range(PAIRS):
                finish(0, c, p, merge([own_part[p], arrived(0, c, p)]))
            send_out(0, c)

        def body(t):
            when_chunk(t + AHEAD, send)
            when_chunk(t + NEAR, send_q)
            when_chunk(t + RELAY, relay)
            when_chunk(t - LAG, middle)
            when_chunk(t - 2 * LAG, close)

        run(2 * LAG, body)
        settle(4, 1)
        for k in range(2):
            flags(k, flag, right).wait_send()

    for g in range(2):
        def done(c, carry, g=g):
            @pl.when(ends(g))
            def _():
                out_local(g, c).wait()

            @pl.when(jnp.logical_not(ends(g)))
            def _():
                out_remote(g, c).wait_send()

            @pl.when(jnp.logical_not(ends(1 - g)))
            def _():
                out_remote(g, c).wait_recv()

            return carry

        lax.fori_loop(0, steps, done, 0)


def solution(mesh):
    sections, spacing = mesh.shape["section"], mesh.shape["ctx"] // 4

    def on_device(dq, dk, dv, uq, uk, uv, key_blocks):
        _, rows, width = dq.shape
        wide = PAIRS * PAIR
        steps = width // wide
        half, full = jnp.bfloat16, jnp.float32
        dma = pltpu.SemaphoreType.DMA
        whole = pl.BlockSpec(memory_space=pl.ANY)
        out = jax.ShapeDtypeStruct(dq.shape, half)

        def body(*refs):
            kernel(sections, spacing, *refs)

        return pl.pallas_call(
            body,
            out_shape=(out, out),
            in_specs=[pl.BlockSpec(memory_space=pltpu.SMEM)] + [whole] * 6,
            out_specs=(whole, whole),
            scratch_shapes=[
                pltpu.VMEM((6, rows, width), half),
                pltpu.VMEM((5, rows, width), half),
                pltpu.VMEM((4, steps, wide, rows), half),
                pltpu.VMEM((4, steps, 4 * PAIRS, rows), full),
                pltpu.VMEM((3, steps, wide, rows), half),
                pltpu.VMEM((3, steps, 4 * PAIRS, rows), full),
                pltpu.VMEM((2, rows, width), half),
                pltpu.VMEM((8, 2 * rows), full),
                pltpu.VMEM((8, 2 * rows), full),
                dma((6,)),
                dma((4, steps)),
                dma((5, steps)),
                dma((3, steps)),
                dma((4, steps)),
                dma((3, steps)),
                dma((4, steps)),
                dma((2, steps)),
                dma((2, steps)),
                dma((2,)),
                dma((1,)),
            ],
            compiler_params=pltpu.CompilerParams(
                collective_id=0, has_side_effects=True, vmem_limit_bytes=67043328),
        )(key_blocks, dq, dk, dv, uq, uk, uv)

    placed = (P("section", "ctx", None),) * 6 + (P("ctx", None),)
    return jax.shard_map(
        on_device,
        mesh=mesh,
        in_specs=placed,
        out_specs=(P("section", "ctx", None), P("section", "ctx", None)),
        check_vma=False,
    )
```

```python
import math

import jax
import jax.numpy as jnp
from jax import lax
from jax.experimental import pallas as pl
from jax.experimental.pallas import tpu as pltpu
from jax.sharding import PartitionSpec as P

HEAD_DIM = 64
PAIR = 2 * HEAD_DIM
PAIRS = 2
AHEAD = 4
RELAY = 2
LAG = 1
NEG = -1e30
FLOOR = -5e29
RATE = math.log2(math.e) / math.sqrt(HEAD_DIM)
MESH = pl.DeviceIdType.MESH


def kernel(sections, spacing, kb, dq, dk, dv, uq, uk, uv, fwd, hand, own, got, part_in, stat_in,
           part_out, stat_out, final, flag, flag_in, load_sem, data_send, data_recv, part_send,
           part_recv, stat_send, stat_recv, out_send, out_recv, flag_send, flag_recv):
    s = lax.axis_index("section")
    i = lax.axis_index("ctx")
    x = i // spacing
    rest = i - x * spacing
    right = (s, lax.rem(x + 1, 4) * spacing + rest)
    left = (s, lax.rem(x + 3, 4) * spacing + rest)
    below = (lax.max(s - 1, 0), i)
    above = (lax.min(s + 1, sections - 1), i)
    rows = own.shape[1]
    wide = PAIRS * PAIR
    steps = own.shape[2] // wide
    ins = (dq, dk, dv, uq, uk, uv)
    QD, KD, VD, QU, KU, VU = range(6)

    def lanes(c):
        return pl.ds(pl.multiple_of(c * wide, wide), wide)

    def remote(src, dst, send, recv, where):
        return pltpu.make_async_remote_copy(
            src_ref=src, dst_ref=dst, send_sem=send, recv_sem=recv, device_id=where,
            device_id_type=MESH)

    def data(k, c, src, r, where):
        return remote(src.at[:, lanes(c)], got.at[r, :, lanes(c)], data_send.at[k, c],
                      data_recv.at[r, c], where)

    def send_in(k, c, a, r, where):
        data(k, c, ins[a].at[0], r, where).start()

    def send_on(k, c, r0, r, where):
        data(k, c, got.at[r0], r, where).start()

    def wait_data(c, *slots):
        for r in slots:
            data(0, c, got.at[r], r, right).wait_recv()

    def parts(k, c, src, stat, r, where):
        return (remote(src.at[c], part_in.at[r, c], part_send.at[k, c], part_recv.at[r, c], where),
                remote(stat.at[c], stat_in.at[r, c], stat_send.at[k, c], stat_recv.at[r, c], where))

    def send_part(k, c, r, where):
        for copy in parts(k, c, part_out.at[k], stat_out.at[k], r, where):
            copy.start()

    def relay_part(k, c, r0, r, where):
        for copy in parts(k, c, part_in.at[r0], stat_in.at[r0], r, where):
            copy.start()

    def wait_part(c, *slots):
        for r in slots:
            for copy in parts(0, c, part_in.at[r], stat_in.at[r], r, right):
                copy.wait_recv()

    def out_remote(g, c):
        src = final.at[g, :, lanes(c)]
        dst = (fwd, hand)[g].at[0, :, lanes(c)]
        return remote(src, dst, out_send.at[g, c], out_recv.at[g, c], (above, below)[g])

    def out_local(g, c):
        dst = (hand, fwd)[g].at[0, :, lanes(c)]
        return pltpu.make_async_copy(final.at[g, :, lanes(c)], dst, out_send.at[g, c])

    def ends(g):
        return s == (sections - 1, 0)[g]

    def send_out(g, c):
        @pl.when(ends(g))
        def _():
            out_local(g, c).start()

        @pl.when(jnp.logical_not(ends(g)))
        def _():
            out_remote(g, c).start()

    lane = lax.broadcasted_iota(jnp.int32, (rows, PAIR), 1)
    row = lax.broadcasted_iota(jnp.int32, (PAIR, rows), 0)
    first = row < HEAD_DIM
    key = lax.broadcasted_iota(jnp.int32, (rows, 2 * rows), 0)
    query = lax.broadcasted_iota(jnp.int32, (rows, 2 * rows), 1)
    causal = key <= lax.rem(query, rows)

    def piece(ref, c, p):
        return ref[:, pl.ds(pl.multiple_of(c * wide + p * PAIR, PAIR), PAIR)]

    def spread(v):
        return jnp.where(first, v[:, :rows], v[:, rows:])

    def attend(q, sources):
        zero = jnp.zeros_like(q)
        both = jnp.concatenate([jnp.where(lane < HEAD_DIM, q, zero), jnp.where(lane < HEAD_DIM, zero, q)], 0)
        tops, scores, floored = [], [], True
        for k, v, bias, masked in sources:
            sc = lax.dot_general(k, both, (((1,), (1,)), ((), ())), preferred_element_type=jnp.float32)
            if masked:
                sc = jnp.where(causal, sc, NEG)
            top = jnp.max(sc, 0, keepdims=True)
            if bias is None:
                floored = False
            else:
                top = top + bias
            tops.append(top)
            scores.append(sc)
        high = tops[0]
        for top in tops[1:]:
            high = jnp.maximum(high, top)
        if floored:
            high = jnp.maximum(high, FLOOR)
        total, mixed = None, None
        for (k, v, bias, masked), sc in zip(sources, scores):
            base = high if bias is None else high - bias
            e = jnp.exp2((sc - base) * RATE)
            t = jnp.sum(e, 0, keepdims=True)
            o = lax.dot_general(v, e.astype(jnp.bfloat16), (((0,), (0,)), ((), ())),
                                preferred_element_type=jnp.float32)
            total = t if total is None else total + t
            mixed = o if mixed is None else mixed + o
        return jnp.where(first, mixed[:, :rows], mixed[:, rows:]), high, total

    def merge(items, floored=False):
        high = items[0][1]
        for item in items[1:]:
            high = jnp.maximum(high, item[1])
        if floored:
            high = jnp.maximum(high, FLOOR)
        mixed, total = None, None
        for o, top, t in items:
            w = jnp.exp2((top - high) * RATE)
            mixed = o * spread(w) if mixed is None else mixed + o * spread(w)
            total = t * w if total is None else total + t * w
        return mixed, high, total

    def keep(k, c, p, item):
        o, top, t = item
        part_out[k, c, pl.ds(p * PAIR, PAIR), :] = o.astype(jnp.bfloat16)
        at = 4 * p
        stat_out[k, c, pl.ds(at, 1), :] = top[:, :rows]
        stat_out[k, c, pl.ds(at + 1, 1), :] = top[:, rows:]
        stat_out[k, c, pl.ds(at + 2, 1), :] = t[:, :rows]
        stat_out[k, c, pl.ds(at + 3, 1), :] = t[:, rows:]

    def arrived(r, c, p, bias=None):
        o = part_in[r, c, pl.ds(p * PAIR, PAIR), :].astype(jnp.float32)
        at = 4 * p
        lines = [stat_in[r, c, pl.ds(at + n, 1), :] for n in range(4)]
        top = jnp.concatenate(lines[:2], 1)
        if bias is not None:
            top = top + bias
        return o, top, jnp.concatenate(lines[2:], 1)

    def finish(g, c, p, item):
        o, top, t = item
        o = o * spread(1.0 / t)
        final[g, :, pl.ds(pl.multiple_of(c * wide + p * PAIR, PAIR), PAIR)] = o.T.astype(jnp.bfloat16)

    def mine(a, c, p):
        return piece(own.at[a], c, p)

    def sent(r, c, p):
        return piece(got.at[r], c, p)

    def self_part(g, c, p):
        q, k, v = (mine(3 * g + n, c, p) for n in range(3))
        return attend(q, [(k, v, None, True)])

    def own_bias(slot):
        return flag[pl.ds(slot, 1), :]

    def far_bias(slot):
        return flag_in[pl.ds(slot, 1), :]

    loads = [pltpu.make_async_copy(ins[a].at[0], own.at[a], load_sem.at[a]) for a in range(6)]
    for copy in loads:
        copy.start()
    bias = [jnp.where(kb[0, n] >= 0, 0.0, NEG) for n in range(2)]
    flag_row = lax.broadcasted_iota(jnp.int32, flag.shape, 0)
    flag[...] = jnp.where(flag_row == 0, bias[0], bias[1])

    barrier = pltpu.get_barrier_semaphore()
    for where in (left, right):
        pl.semaphore_signal(barrier, inc=1, device_id=where, device_id_type=MESH)

    @pl.when(s > 0)
    def _():
        pl.semaphore_signal(barrier, inc=1, device_id=below, device_id_type=MESH)

    @pl.when(s < sections - 1)
    def _():
        pl.semaphore_signal(barrier, inc=1, device_id=above, device_id_type=MESH)

    edges = jnp.where(s > 0, 1, 0) + jnp.where(s < sections - 1, 1, 0)
    pl.semaphore_wait(barrier, 2 + edges)

    def flags(k, src, where):
        return remote(src, flag_in, flag_send.at[k], flag_recv.at[0], where)

    def wait_loads():
        for copy in loads:
            copy.wait()

    def ahead(send):
        def go(c, carry):
            send(c)
            return carry

        lax.fori_loop(0, min(AHEAD, steps), go, 0)

    def run(extra, body):
        def go(t, carry):
            body(t)
            return carry

        lax.fori_loop(0, steps + extra, go, 0)

    def when_chunk(c, act):
        @pl.when(jnp.logical_and(c >= 0, c < steps))
        def _():
            act(c)

    def settle(n_data, n_part):
        def go(c, carry):
            for k in range(n_data):
                data(k, c, got.at[0], 0, right).wait_send()
            for k in range(n_part):
                for copy in parts(k, c, part_out.at[k], stat_out.at[k], 0, right):
                    copy.wait_send()
            return carry

        lax.fori_loop(0, steps, go, 0)

    @pl.when(x == 0)
    def _():
        def send(c):
            send_in(0, c, KD, 0, right)
            send_in(1, c, VD, 1, right)

        ahead(send)
        wait_loads()
        flags(0, flag, right).wait_recv()

        def hub(c):
            wait_data(c, 0, 1, 2, 3, 4)
            for p in range(PAIRS):
                k0, v0 = mine(KU, c, p), mine(VU, c, p)
                k1, v1 = sent(0, c, p), sent(1, c, p)
                keep(1, c, p, attend(sent(3, c, p), [(k1, v1, far_bias(0), False), (k0, v0, far_bias(1), False)]))
            send_part(1, c, 3, left)
            for p in range(PAIRS):
                keep(2, c, p, attend(sent(4, c, p), [(sent(0, c, p), sent(1, c, p), None, False)]))
            send_part(2, c, 2, left)
            for p in range(PAIRS):
                keep(0, c, p, attend(sent(2, c, p), [(mine(KU, c, p), mine(VU, c, p), None, False)]))
            send_part(0, c, 0, right)
            for p in range(PAIRS):
                finish(1, c, p, self_part(1, c, p))
                finish(0, c, p, self_part(0, c, p))
            send_out(1, c)
            send_out(0, c)

        def body(t):
            when_chunk(t + AHEAD, send)
            hub(t)

        run(0, body)
        settle(2, 3)

    @pl.when(x == 1)
    def _():
        def send(c):
            send_in(0, c, KU, 0, left)
            send_in(1, c, VU, 1, left)
            send_in(2, c, QU, 2, left)

        ahead(send)
        wait_loads()
        flags(0, flag, right).wait_recv()

        def hub(c):
            wait_data(c, 0, 1, 2, 3)
            for p in range(PAIRS):
                keep(1, c, p, attend(sent(3, c, p), [(mine(KD, c, p), mine(VD, c, p), None, False)]))
            send_part(1, c, 1, right)
            for p in range(PAIRS):
                k1, v1 = mine(KD, c, p), mine(VD, c, p)
                k0, v0 = sent(0, c, p), sent(1, c, p)
                keep(0, c, p, attend(sent(2, c, p), [(k1, v1, far_bias(0), False), (k0, v0, far_bias(1), False)]))
            send_part(0, c, 0, right)
            for p in range(PAIRS):
                k1, v1 = mine(KD, c, p), mine(VD, c, p)
                k0, v0 = sent(0, c, p), sent(1, c, p)
                finish(0, c, p, attend(mine(QD, c, p), [(k1, v1, None, True), (k0, v0, own_bias(0), False)]))
            send_out(0, c)

        def close(c):
            own_part = [self_part(1, c, p) for p in range(PAIRS)]
            wait_part(c, 0)
            for p in range(PAIRS):
                finish(1, c, p, merge([own_part[p], arrived(0, c, p, own_bias(0))]))
            send_out(1, c)

        def body(t):
            when_chunk(t + AHEAD, send)
            when_chunk(t, hub)
            when_chunk(t - LAG, close)

        run(LAG, body)
        settle(3, 2)

    @pl.when(x == 2)
    def _():
        flags(0, flag, left).start()
        flags(1, flag, right).start()

        def send(c):
            send_in(0, c, QD, 2, left)
            send_in(1, c, QU, 0, right)

        ahead(send)

        def relay(c):
            wait_data(c, 0)
            send_on(2, c, 0, 3, left)

        for c in range(min(RELAY, steps)):
            relay(c)
        wait_loads()
        flags(0, flag, right).wait_recv()

        def side(c):
            wait_data(c, 1)
            for p in range(PAIRS):
                keep(1, c, p, attend(sent(1, c, p), [(mine(KU, c, p), mine(VU, c, p), None, False)]))
            send_part(1, c, 1, right)

        def middle(c):
            near = [attend(sent(0, c, p), [(mine(KD, c, p), mine(VD, c, p), far_bias(0), False)])
                    for p in range(PAIRS)]
            wait_part(c, 1)
            for p in range(PAIRS):
                keep(0, c, p, merge([near[p], arrived(1, c, p, far_bias(1))], True))
            send_part(0, c, 0, right)
            own_part = [self_part(0, c, p) for p in range(PAIRS)]
            wait_part(c, 0)
            for p in range(PAIRS):
                finish(0, c, p, merge([own_part[p], arrived(0, c, p)]))
            send_out(0, c)

        def close(c):
            own_part = [self_part(1, c, p) for p in range(PAIRS)]
            wait_part(c, 2)
            for p in range(PAIRS):
                finish(1, c, p, merge([own_part[p], arrived(2, c, p)]))
            send_out(1, c)

        def body(t):
            when_chunk(t + AHEAD, send)
            when_chunk(t + RELAY, relay)
            when_chunk(t, side)
            when_chunk(t - LAG, middle)
            when_chunk(t - 2 * LAG, close)

        run(2 * LAG, body)
        settle(3, 2)
        for k in range(2):
            flags(k, flag, right).wait_send()

    @pl.when(x == 3)
    def _():
        flags(0, flag, left).start()

        def send(c):
            send_in(0, c, QD, 0, left)
            send_in(1, c, QU, 1, left)
            send_in(2, c, QU, 4, right)

        ahead(send)
        flags(0, flag, right).wait_recv()
        flags(1, flag_in, right).start()

        def relay(c):
            wait_data(c, 0)
            send_on(3, c, 0, 3, right)

        for c in range(min(RELAY, steps)):
            relay(c)
        wait_loads()

        def middle(c):
            wait_part(c, 3)
            relay_part(0, c, 3, 2, left)
            own_part = [self_part(1, c, p) for p in range(PAIRS)]
            wait_part(c, 1, 2)
            for p in range(PAIRS):
                items = [own_part[p], arrived(1, c, p, own_bias(0)), arrived(2, c, p, own_bias(1))]
                finish(1, c, p, merge(items))
            send_out(1, c)

        def close(c):
            own_part = [self_part(0, c, p) for p in range(PAIRS)]
            wait_part(c, 0)
            for p in range(PAIRS):
                finish(0, c, p, merge([own_part[p], arrived(0, c, p)]))
            send_out(0, c)

        def body(t):
            when_chunk(t + AHEAD, send)
            when_chunk(t + RELAY, relay)
            when_chunk(t - LAG, middle)
            when_chunk(t - 2 * LAG, close)

        run(2 * LAG, body)
        settle(4, 1)
        for k in range(2):
            flags(k, flag, right).wait_send()

    for g in range(2):
        def done(c, carry, g=g):
            @pl.when(ends(g))
            def _():
                out_local(g, c).wait()

            @pl.when(jnp.logical_not(ends(g)))
            def _():
                out_remote(g, c).wait_send()

            @pl.when(jnp.logical_not(ends(1 - g)))
            def _():
                out_remote(g, c).wait_recv()

            return carry

        lax.fori_loop(0, steps, done, 0)


def solution(mesh):
    sections, spacing = mesh.shape["section"], mesh.shape["ctx"] // 4

    def on_device(dq, dk, dv, uq, uk, uv, key_blocks):
        _, rows, width = dq.shape
        wide = PAIRS * PAIR
        steps = width // wide
        half, full = jnp.bfloat16, jnp.float32
        dma = pltpu.SemaphoreType.DMA
        whole = pl.BlockSpec(memory_space=pl.ANY)
        out = pltpu.VMEM(dq.shape, half)

        def body(*refs):
            kernel(sections, spacing, *refs)

        return pl.pallas_call(
            body,
            out_shape=(out, out),
            in_specs=[pl.BlockSpec(memory_space=pltpu.SMEM)] + [whole] * 6,
            out_specs=(whole, whole),
            scratch_shapes=[
                pltpu.VMEM((6, rows, width), half),
                pltpu.VMEM((5, rows, width), half),
                pltpu.VMEM((4, steps, wide, rows), half),
                pltpu.VMEM((4, steps, 4 * PAIRS, rows), full),
                pltpu.VMEM((3, steps, wide, rows), half),
                pltpu.VMEM((3, steps, 4 * PAIRS, rows), full),
                pltpu.VMEM((2, rows, width), half),
                pltpu.VMEM((8, 2 * rows), full),
                pltpu.VMEM((8, 2 * rows), full),
                dma((6,)),
                dma((4, steps)),
                dma((5, steps)),
                dma((3, steps)),
                dma((4, steps)),
                dma((3, steps)),
                dma((4, steps)),
                dma((2, steps)),
                dma((2, steps)),
                dma((2,)),
                dma((1,)),
            ],
            compiler_params=pltpu.CompilerParams(
                collective_id=0, has_side_effects=True, vmem_limit_bytes=62000000),
        )(key_blocks, dq, dk, dv, uq, uk, uv)

    placed = (P("section", "ctx", None),) * 6 + (P("ctx", None),)
    return jax.shard_map(
        on_device,
        mesh=mesh,
        in_specs=placed,
        out_specs=(P("section", "ctx", None), P("section", "ctx", None)),
        check_vma=False,
    )
```

```python
import math

import jax
import jax.numpy as jnp
from jax import lax
from jax.experimental import pallas as pl
from jax.experimental.pallas import tpu as pltpu
from jax.sharding import PartitionSpec as P

HEAD_DIM = 64
PAIR = 2 * HEAD_DIM
PAIRS = 1
AHEAD = 6
RELAY = 3
LAG = 2
NEG = -1e30
FLOOR = -5e29
RATE = math.log2(math.e) / math.sqrt(HEAD_DIM)
MESH = pl.DeviceIdType.MESH


def kernel(sections, spacing, kb, dq, dk, dv, uq, uk, uv, fwd, hand, own, got, part_in, stat_in,
           part_out, stat_out, final, flag, flag_in, load_sem, data_send, data_recv, part_send,
           part_recv, stat_send, stat_recv, out_send, out_recv, flag_send, flag_recv):
    s = lax.axis_index("section")
    i = lax.axis_index("ctx")
    x = i // spacing
    rest = i - x * spacing
    right = (s, lax.rem(x + 1, 4) * spacing + rest)
    left = (s, lax.rem(x + 3, 4) * spacing + rest)
    below = (lax.max(s - 1, 0), i)
    above = (lax.min(s + 1, sections - 1), i)
    rows = own.shape[1]
    wide = PAIRS * PAIR
    steps = own.shape[2] // wide
    ins = (dq, dk, dv, uq, uk, uv)
    QD, KD, VD, QU, KU, VU = range(6)

    def lanes(c):
        return pl.ds(pl.multiple_of(c * wide, wide), wide)

    def remote(src, dst, send, recv, where):
        return pltpu.make_async_remote_copy(
            src_ref=src, dst_ref=dst, send_sem=send, recv_sem=recv, device_id=where,
            device_id_type=MESH)

    def data(k, c, src, r, where):
        return remote(src.at[:, lanes(c)], got.at[r, :, lanes(c)], data_send.at[k, c],
                      data_recv.at[r, c], where)

    def send_in(k, c, a, r, where):
        data(k, c, ins[a].at[0], r, where).start()

    def send_on(k, c, r0, r, where):
        data(k, c, got.at[r0], r, where).start()

    def wait_data(c, *slots):
        for r in slots:
            data(0, c, got.at[r], r, right).wait_recv()

    def parts(k, c, src, stat, r, where):
        return (remote(src.at[c], part_in.at[r, c], part_send.at[k, c], part_recv.at[r, c], where),
                remote(stat.at[c], stat_in.at[r, c], stat_send.at[k, c], stat_recv.at[r, c], where))

    def send_part(k, c, r, where):
        for copy in parts(k, c, part_out.at[k], stat_out.at[k], r, where):
            copy.start()

    def relay_part(k, c, r0, r, where):
        for copy in parts(k, c, part_in.at[r0], stat_in.at[r0], r, where):
            copy.start()

    def wait_part(c, *slots):
        for r in slots:
            for copy in parts(0, c, part_in.at[r], stat_in.at[r], r, right):
                copy.wait_recv()

    def out_remote(g, c):
        src = final.at[g, :, lanes(c)]
        dst = (fwd, hand)[g].at[0, :, lanes(c)]
        return remote(src, dst, out_send.at[g, c], out_recv.at[g, c], (above, below)[g])

    def out_local(g, c):
        dst = (hand, fwd)[g].at[0, :, lanes(c)]
        return pltpu.make_async_copy(final.at[g, :, lanes(c)], dst, out_send.at[g, c])

    def ends(g):
        return s == (sections - 1, 0)[g]

    def send_out(g, c):
        @pl.when(ends(g))
        def _():
            out_local(g, c).start()

        @pl.when(jnp.logical_not(ends(g)))
        def _():
            out_remote(g, c).start()

    lane = lax.broadcasted_iota(jnp.int32, (rows, PAIR), 1)
    row = lax.broadcasted_iota(jnp.int32, (PAIR, rows), 0)
    first = row < HEAD_DIM
    key = lax.broadcasted_iota(jnp.int32, (rows, 2 * rows), 0)
    query = lax.broadcasted_iota(jnp.int32, (rows, 2 * rows), 1)
    causal = key <= lax.rem(query, rows)

    def piece(ref, c, p):
        return ref[:, pl.ds(pl.multiple_of(c * wide + p * PAIR, PAIR), PAIR)]

    def spread(v):
        return jnp.where(first, v[:, :rows], v[:, rows:])

    def attend(q, sources):
        zero = jnp.zeros_like(q)
        both = jnp.concatenate([jnp.where(lane < HEAD_DIM, q, zero), jnp.where(lane < HEAD_DIM, zero, q)], 0)
        tops, scores, floored = [], [], True
        for k, v, bias, masked in sources:
            sc = lax.dot_general(k, both, (((1,), (1,)), ((), ())), preferred_element_type=jnp.float32)
            if masked:
                sc = jnp.where(causal, sc, NEG)
            top = jnp.max(sc, 0, keepdims=True)
            if bias is None:
                floored = False
            else:
                top = top + bias
            tops.append(top)
            scores.append(sc)
        high = tops[0]
        for top in tops[1:]:
            high = jnp.maximum(high, top)
        if floored:
            high = jnp.maximum(high, FLOOR)
        total, mixed = None, None
        for (k, v, bias, masked), sc in zip(sources, scores):
            base = high if bias is None else high - bias
            e = jnp.exp2((sc - base) * RATE)
            t = jnp.sum(e, 0, keepdims=True)
            o = lax.dot_general(v, e.astype(jnp.bfloat16), (((0,), (0,)), ((), ())),
                                preferred_element_type=jnp.float32)
            total = t if total is None else total + t
            mixed = o if mixed is None else mixed + o
        return jnp.where(first, mixed[:, :rows], mixed[:, rows:]), high, total

    def merge(items, floored=False):
        high = items[0][1]
        for item in items[1:]:
            high = jnp.maximum(high, item[1])
        if floored:
            high = jnp.maximum(high, FLOOR)
        mixed, total = None, None
        for o, top, t in items:
            w = jnp.exp2((top - high) * RATE)
            mixed = o * spread(w) if mixed is None else mixed + o * spread(w)
            total = t * w if total is None else total + t * w
        return mixed, high, total

    def keep(k, c, p, item):
        o, top, t = item
        part_out[k, c, pl.ds(p * PAIR, PAIR), :] = o.astype(jnp.bfloat16)
        at = 4 * p
        stat_out[k, c, pl.ds(at, 1), :] = top[:, :rows]
        stat_out[k, c, pl.ds(at + 1, 1), :] = top[:, rows:]
        stat_out[k, c, pl.ds(at + 2, 1), :] = t[:, :rows]
        stat_out[k, c, pl.ds(at + 3, 1), :] = t[:, rows:]

    def arrived(r, c, p, bias=None):
        o = part_in[r, c, pl.ds(p * PAIR, PAIR), :].astype(jnp.float32)
        at = 4 * p
        lines = [stat_in[r, c, pl.ds(at + n, 1), :] for n in range(4)]
        top = jnp.concatenate(lines[:2], 1)
        if bias is not None:
            top = top + bias
        return o, top, jnp.concatenate(lines[2:], 1)

    def finish(g, c, p, item):
        o, top, t = item
        o = o * spread(1.0 / t)
        final[g, :, pl.ds(pl.multiple_of(c * wide + p * PAIR, PAIR), PAIR)] = o.T.astype(jnp.bfloat16)

    def mine(a, c, p):
        return piece(own.at[a], c, p)

    def sent(r, c, p):
        return piece(got.at[r], c, p)

    def self_part(g, c, p):
        q, k, v = (mine(3 * g + n, c, p) for n in range(3))
        return attend(q, [(k, v, None, True)])

    def own_bias(slot):
        return flag[pl.ds(slot, 1), :]

    def far_bias(slot):
        return flag_in[pl.ds(slot, 1), :]

    loads = [pltpu.make_async_copy(ins[a].at[0], own.at[a], load_sem.at[a]) for a in range(6)]
    for copy in loads:
        copy.start()
    bias = [jnp.where(kb[0, n] >= 0, 0.0, NEG) for n in range(2)]
    flag_row = lax.broadcasted_iota(jnp.int32, flag.shape, 0)
    flag[...] = jnp.where(flag_row == 0, bias[0], bias[1])

    barrier = pltpu.get_barrier_semaphore()
    for where in (left, right):
        pl.semaphore_signal(barrier, inc=1, device_id=where, device_id_type=MESH)

    @pl.when(s > 0)
    def _():
        pl.semaphore_signal(barrier, inc=1, device_id=below, device_id_type=MESH)

    @pl.when(s < sections - 1)
    def _():
        pl.semaphore_signal(barrier, inc=1, device_id=above, device_id_type=MESH)

    edges = jnp.where(s > 0, 1, 0) + jnp.where(s < sections - 1, 1, 0)
    pl.semaphore_wait(barrier, 2 + edges)

    def flags(k, src, where):
        return remote(src, flag_in, flag_send.at[k], flag_recv.at[0], where)

    def wait_loads():
        for copy in loads:
            copy.wait()

    def ahead(send):
        def go(c, carry):
            send(c)
            return carry

        lax.fori_loop(0, min(AHEAD, steps), go, 0)

    def run(extra, body):
        def go(t, carry):
            body(t)
            return carry

        lax.fori_loop(0, steps + extra, go, 0)

    def when_chunk(c, act):
        @pl.when(jnp.logical_and(c >= 0, c < steps))
        def _():
            act(c)

    def settle(n_data, n_part):
        def go(c, carry):
            for k in range(n_data):
                data(k, c, got.at[0], 0, right).wait_send()
            for k in range(n_part):
                for copy in parts(k, c, part_out.at[k], stat_out.at[k], 0, right):
                    copy.wait_send()
            return carry

        lax.fori_loop(0, steps, go, 0)

    @pl.when(x == 0)
    def _():
        def send(c):
            send_in(0, c, KD, 0, right)
            send_in(1, c, VD, 1, right)

        ahead(send)
        wait_loads()
        flags(0, flag, right).wait_recv()

        def hub(c):
            wait_data(c, 0, 1, 2, 3, 4)
            for p in range(PAIRS):
                k0, v0 = mine(KU, c, p), mine(VU, c, p)
                k1, v1 = sent(0, c, p), sent(1, c, p)
                keep(1, c, p, attend(sent(3, c, p), [(k1, v1, far_bias(0), False), (k0, v0, far_bias(1), False)]))
            send_part(1, c, 3, left)
            for p in range(PAIRS):
                keep(2, c, p, attend(sent(4, c, p), [(sent(0, c, p), sent(1, c, p), None, False)]))
            send_part(2, c, 2, left)
            for p in range(PAIRS):
                keep(0, c, p, attend(sent(2, c, p), [(mine(KU, c, p), mine(VU, c, p), None, False)]))
            send_part(0, c, 0, right)
            for p in range(PAIRS):
                finish(1, c, p, self_part(1, c, p))
                finish(0, c, p, self_part(0, c, p))
            send_out(1, c)
            send_out(0, c)

        def body(t):
            when_chunk(t + AHEAD, send)
            hub(t)

        run(0, body)
        settle(2, 3)

    @pl.when(x == 1)
    def _():
        def send(c):
            send_in(0, c, KU, 0, left)
            send_in(1, c, VU, 1, left)
            send_in(2, c, QU, 2, left)

        ahead(send)
        wait_loads()
        flags(0, flag, right).wait_recv()

        def hub(c):
            wait_data(c, 0, 1, 2, 3)
            for p in range(PAIRS):
                keep(1, c, p, attend(sent(3, c, p), [(mine(KD, c, p), mine(VD, c, p), None, False)]))
            send_part(1, c, 1, right)
            for p in range(PAIRS):
                k1, v1 = mine(KD, c, p), mine(VD, c, p)
                k0, v0 = sent(0, c, p), sent(1, c, p)
                keep(0, c, p, attend(sent(2, c, p), [(k1, v1, far_bias(0), False), (k0, v0, far_bias(1), False)]))
            send_part(0, c, 0, right)
            for p in range(PAIRS):
                k1, v1 = mine(KD, c, p), mine(VD, c, p)
                k0, v0 = sent(0, c, p), sent(1, c, p)
                finish(0, c, p, attend(mine(QD, c, p), [(k1, v1, None, True), (k0, v0, own_bias(0), False)]))
            send_out(0, c)

        def close(c):
            own_part = [self_part(1, c, p) for p in range(PAIRS)]
            wait_part(c, 0)
            for p in range(PAIRS):
                finish(1, c, p, merge([own_part[p], arrived(0, c, p, own_bias(0))]))
            send_out(1, c)

        def body(t):
            when_chunk(t + AHEAD, send)
            when_chunk(t, hub)
            when_chunk(t - LAG, close)

        run(LAG, body)
        settle(3, 2)

    @pl.when(x == 2)
    def _():
        flags(0, flag, left).start()
        flags(1, flag, right).start()

        def send(c):
            send_in(0, c, QD, 2, left)
            send_in(1, c, QU, 0, right)

        ahead(send)

        def relay(c):
            wait_data(c, 0)
            send_on(2, c, 0, 3, left)

        for c in range(min(RELAY, steps)):
            relay(c)
        wait_loads()
        flags(0, flag, right).wait_recv()

        def side(c):
            wait_data(c, 1)
            for p in range(PAIRS):
                keep(1, c, p, attend(sent(1, c, p), [(mine(KU, c, p), mine(VU, c, p), None, False)]))
            send_part(1, c, 1, right)

        def middle(c):
            near = [attend(sent(0, c, p), [(mine(KD, c, p), mine(VD, c, p), far_bias(0), False)])
                    for p in range(PAIRS)]
            wait_part(c, 1)
            for p in range(PAIRS):
                keep(0, c, p, merge([near[p], arrived(1, c, p, far_bias(1))], True))
            send_part(0, c, 0, right)
            own_part = [self_part(0, c, p) for p in range(PAIRS)]
            wait_part(c, 0)
            for p in range(PAIRS):
                finish(0, c, p, merge([own_part[p], arrived(0, c, p)]))
            send_out(0, c)

        def close(c):
            own_part = [self_part(1, c, p) for p in range(PAIRS)]
            wait_part(c, 2)
            for p in range(PAIRS):
                finish(1, c, p, merge([own_part[p], arrived(2, c, p)]))
            send_out(1, c)

        def body(t):
            when_chunk(t + AHEAD, send)
            when_chunk(t + RELAY, relay)
            when_chunk(t, side)
            when_chunk(t - 2 * LAG, close)
            when_chunk(t - LAG, middle)

        run(2 * LAG, body)
        settle(3, 2)
        for k in range(2):
            flags(k, flag, right).wait_send()

    @pl.when(x == 3)
    def _():
        flags(0, flag, left).start()

        def send(c):
            send_in(0, c, QD, 0, left)
            send_in(1, c, QU, 1, left)
            send_in(2, c, QU, 4, right)

        ahead(send)
        flags(0, flag, right).wait_recv()
        flags(1, flag_in, right).start()

        def relay(c):
            wait_data(c, 0)
            send_on(3, c, 0, 3, right)

        for c in range(min(RELAY, steps)):
            relay(c)
        wait_loads()

        def middle(c):
            wait_part(c, 3)
            relay_part(0, c, 3, 2, left)
            own_part = [self_part(1, c, p) for p in range(PAIRS)]
            wait_part(c, 1, 2)
            for p in range(PAIRS):
                items = [own_part[p], arrived(1, c, p, own_bias(0)), arrived(2, c, p, own_bias(1))]
                finish(1, c, p, merge(items))
            send_out(1, c)

        def close(c):
            own_part = [self_part(0, c, p) for p in range(PAIRS)]
            wait_part(c, 0)
            for p in range(PAIRS):
                finish(0, c, p, merge([own_part[p], arrived(0, c, p)]))
            send_out(0, c)

        def body(t):
            when_chunk(t + AHEAD, send)
            when_chunk(t + RELAY, relay)
            when_chunk(t - LAG, middle)
            when_chunk(t - 2 * LAG, close)

        run(2 * LAG, body)
        settle(4, 1)
        for k in range(2):
            flags(k, flag, right).wait_send()

    for g in range(2):
        def done(c, carry, g=g):
            @pl.when(ends(g))
            def _():
                out_local(g, c).wait()

            @pl.when(jnp.logical_not(ends(g)))
            def _():
                out_remote(g, c).wait_send()

            @pl.when(jnp.logical_not(ends(1 - g)))
            def _():
                out_remote(g, c).wait_recv()

            return carry

        lax.fori_loop(0, steps, done, 0)


def solution(mesh):
    sections, spacing = mesh.shape["section"], mesh.shape["ctx"] // 4

    def on_device(dq, dk, dv, uq, uk, uv, key_blocks):
        _, rows, width = dq.shape
        wide = PAIRS * PAIR
        steps = width // wide
        half, full = jnp.bfloat16, jnp.float32
        dma = pltpu.SemaphoreType.DMA
        whole = pl.BlockSpec(memory_space=pl.ANY)
        out = pltpu.VMEM(dq.shape, half)

        def body(*refs):
            kernel(sections, spacing, *refs)

        return pl.pallas_call(
            body,
            out_shape=(out, out),
            in_specs=[pl.BlockSpec(memory_space=pltpu.SMEM)] + [whole] * 6,
            out_specs=(whole, whole),
            scratch_shapes=[
                pltpu.VMEM((6, rows, width), half),
                pltpu.VMEM((5, rows, width), half),
                pltpu.VMEM((4, steps, wide, rows), half),
                pltpu.VMEM((4, steps, 4 * PAIRS, rows), full),
                pltpu.VMEM((3, steps, wide, rows), half),
                pltpu.VMEM((3, steps, 4 * PAIRS, rows), full),
                pltpu.VMEM((2, rows, width), half),
                pltpu.VMEM((8, 2 * rows), full),
                pltpu.VMEM((8, 2 * rows), full),
                dma((6,)),
                dma((4, steps)),
                dma((5, steps)),
                dma((3, steps)),
                dma((4, steps)),
                dma((3, steps)),
                dma((4, steps)),
                dma((2, steps)),
                dma((2, steps)),
                dma((2,)),
                dma((1,)),
            ],
            compiler_params=pltpu.CompilerParams(
                collective_id=0, has_side_effects=True, vmem_limit_bytes=62000000),
        )(key_blocks, dq, dk, dv, uq, uk, uv)

    placed = (P("section", "ctx", None),) * 6 + (P("ctx", None),)
    return jax.shard_map(
        on_device,
        mesh=mesh,
        in_specs=placed,
        out_specs=(P("section", "ctx", None), P("section", "ctx", None)),
        check_vma=False,
    )
```
